32 devices in a mesh: sec: 2 (over y), gy: 4 (over z), gx: 4 (over x, core).
Axes of the slice: x: 2, y: 2, z: 4, core: 2. Of those that a mesh axis runs over, the one named last changes fastest.
Arguments:
- ocean: bfloat16 [32, 3, 1024, 1536], P(('sec', 'gy'), None, None, 'gx'), may hold values from -6 to 6
- level_weight: float32 [32], replicated, may hold values from 0.25 to 2.5
- velocity_start: float32 [2, 1024, 1536], P(None, ('sec', 'gy'), 'gx'), may hold values from -3 to 3
- wind_stress: float32 [2, 1024, 1536], P(None, ('sec', 'gy'), 'gx'), may hold values from -3 to 3
- thickness: float32 [1024, 1536], P(('sec', 'gy'), 'gx'), may hold values from 0.5 to 2.5
- concentration: float32 [1024, 1536], P(('sec', 'gy'), 'gx'), may hold values from 0.3 to 1
- ice_mask: int32 [1024, 1536], P(('sec', 'gy'), 'gx'), may hold values 0 or 1
- land_mask: int32 [1024, 1536], P(('sec', 'gy'), 'gx'), may hold values 0 or 1
Outputs:
- ice_velocity: float32 [2, 1024, 1536], P(None, ('sec', 'gy'), 'gx')
- ice_stress: float32 [3, 1024, 1536], P(None, ('sec', 'gy'), 'gx')
The draws below stay inside these ranges and needn't reach their ends.
All inputs are finite; a program needn't handle non-finite values. No bound on the sum of `ice_mask` or of `land_mask` on one device may be relied on, other than what follows from the above.
Results may differ from the reference program's by a relative error of at most 0.0003.
Values may be sent and summed in bfloat16 or wider, within the bound.
A program may use at most 128 MiB of HBM per device.

```python
import math
import jax
import jax.numpy as jnp
from jax import lax

SUB = 4
LEV = 32
NY = 1024
NX = 1536


def place_ends(array, rng, least, largest):
    dims = array.shape
    index_at = [jax.random.randint(jax.random.fold_in(rng, axis), (), 0, dims[axis]) for axis in range(len(dims))]
    array = array.at[tuple(index_at)].set(least)
    longest = dims.index(max(dims))
    index_at[longest] = (index_at[longest] + 1) % dims[longest]
    return array.at[tuple(index_at)].set(largest)


def with_spikes(result, rng, source, target, blocks, factor):
    def block_of(axis_at):
        return (jnp.arange(result.shape[axis_at]) // (result.shape[axis_at] // blocks)).reshape((-1,) + (1,) * (result.ndim - 1 - axis_at))

    first = jax.random.permutation(rng, blocks)[block_of(target)]
    far = (block_of(target) + blocks // 2) % blocks
    return jnp.where((block_of(source) == first) | (block_of(source) == far), factor * result, result)


def block_levels(key, dims, pieces, least, high):
    loudness = 1.0
    for axis_at, parts in pieces:
        heights = jax.random.uniform(jax.random.fold_in(jax.random.fold_in(key, 6), axis_at), (parts,), jnp.float32, least / len(pieces), high / len(pieces))
        loudness = loudness * jnp.repeat(jnp.exp(heights), dims[axis_at] // parts).reshape((-1,) + (1,) * (len(dims) - 1 - axis_at))
    return loudness


def normal_values(own_key, shape, scale, limit, shards=(), held_as=jnp.bfloat16):
    array = jax.random.normal(own_key, shape, jnp.float32) * scale
    if len(shards) > 0:
        array = block_levels(own_key, shape, shards, -0.22, 0.18) * array
    return jnp.clip(array, min=-limit, max=limit).astype(held_as)


def noise_with(rng, shape, deviation, most, cuts, heavy, held_as=jnp.bfloat16):
    drawn = deviation * jax.random.normal(rng, shape, jnp.float32)
    if cuts:
        drawn = drawn * block_levels(rng, shape, cuts, -0.22, 0.18)
    return jnp.clip(with_spikes(drawn, jax.random.fold_in(rng, 3), *heavy), -most, most).astype(held_as)


def setup_inputs(seed: int = 0) -> dict:
    arg_keys = jax.random.split(jax.random.key(seed), 9)
    ocean = noise_with(arg_keys[0], (LEV, 3, NY, NX), 1.0, 6.0, ((0, 8), (3, 4)), (0, 2, 8, 2.0))
    level_weight = jnp.clip(jnp.exp(jax.random.uniform(arg_keys[1], (LEV,), jnp.float32, math.log(0.25), math.log(2.5))), 0.25, 2.5)
    velocity_start = normal_values(arg_keys[2], (2, NY, NX), 0.5, 3.0, ((1, 8), (2, 4)), jnp.float32)
    wind_stress = normal_values(arg_keys[3], (2, NY, NX), 0.4, 3.0, ((1, 8), (2, 4)), jnp.float32)
    thickness = jnp.clip(0.5 + 2.0 * jax.random.uniform(arg_keys[4], (NY, NX), jnp.float32) ** block_levels(arg_keys[4], (NY, NX), ((0, 8), (1, 4)), -0.2, 0.2), 0.5, 2.5)
    concentration = jnp.clip(0.3 + 0.7 * jax.random.uniform(arg_keys[5], (NY, NX), jnp.float32) ** block_levels(arg_keys[5], (NY, NX), ((0, 8), (1, 4)), -0.2, 0.2), 0.3, 1.0)
    ice_mask = place_ends((jax.random.randint(arg_keys[6], (NY, NX), 0, 4) < 3).astype(jnp.int32), jax.random.fold_in(arg_keys[6], 1), 0, 1)
    land_mask = place_ends((jax.random.randint(arg_keys[7], (NY, NX), 0, 10) < 9).astype(jnp.int32), jax.random.fold_in(arg_keys[7], 1), 0, 1)
    return {"ocean": ocean, "level_weight": level_weight, "velocity_start": velocity_start, "wind_stress": wind_stress, "thickness": thickness, "concentration": concentration, "ice_mask": ice_mask, "land_mask": land_mask}


ecc_square = 4.0
strain_floor = 0.01
relax_rate = 0.5
water_drag = 0.8
coriolis_f = 0.5
slope_gain = 0.5
conc_decay = 4.0

def centre_x(field):
    return 0.5 * (field[..., 1:-1, 2:] - field[..., 1:-1, :-2])

def centre_y(field):
    return 0.5 * (field[..., 2:, 1:-1] - field[..., :-2, 1:-1])

def stresses(velocity, stress, strength, covered):
    east_u = centre_x(velocity[0])
    north_v = centre_y(velocity[1])
    north_u = centre_y(velocity[0])
    east_v = centre_x(velocity[1])
    spread = east_u + north_v
    tension = east_u - north_v
    shear = north_u + east_v
    delta = jnp.sqrt(spread * spread + (tension * tension + shear * shear) / ecc_square + strain_floor)
    first = (stress[0] + relax_rate * (strength * spread / delta - strength)) / (1.0 + relax_rate)
    second = (stress[1] + relax_rate * strength * tension / (ecc_square * delta)) / (1.0 + relax_rate)
    third = (stress[2] + relax_rate * strength * shear / (2.0 * ecc_square * delta)) / (1.0 + relax_rate)
    return jnp.stack([first, second, third]) * covered

def slope_force(height):
    return -slope_gain * jnp.stack([centre_x(height), centre_y(height)])

def momentum(velocity, stress, ice_mass, current, slope, wind_drag, moving):
    normal_x = 0.5 * (stress[0] + stress[1])
    normal_y = 0.5 * (stress[0] - stress[1])
    force_x = centre_x(normal_x) + centre_y(stress[2])
    force_y = centre_x(stress[2]) + centre_y(normal_y)
    rel_u = current[0] - velocity[0]
    rel_v = current[1] - velocity[1]
    drag = water_drag * jnp.sqrt(rel_u * rel_u + rel_v * rel_v)
    diagonal = ice_mass + drag
    turning = coriolis_f * ice_mass
    right_x = ice_mass * velocity[0] + force_x + drag * current[0] + wind_drag[0] + ice_mass * slope[0]
    right_y = ice_mass * velocity[1] + force_y + drag * current[1] + wind_drag[1] + ice_mass * slope[1]
    live = moving > 0.5
    denom = jnp.where(live, diagonal * diagonal + turning * turning, 1.0)
    new_u = jnp.where(live, (diagonal * right_x + turning * right_y) / denom, 0.0)
    new_v = jnp.where(live, (diagonal * right_y - turning * right_x) / denom, 0.0)
    return jnp.stack([new_u, new_v])

def extend(field, width):
    wide = jnp.concatenate([field[:, :, -width:], field, field[:, :, :width]], axis=2)
    return jnp.pad(wide, ((0, 0), (width, width), (0, 0)))

def reference(ocean, level_weight, velocity_start, wind_stress, thickness, concentration, ice_mask, land_mask):

    def add_level(level, total):
        return total + level_weight[level] * ocean[level].astype(jnp.float32)
    total = lax.fori_loop(0, LEV, add_level, jnp.zeros((3, NY, NX), jnp.float32))
    surface = total / math.sqrt(LEV)
    strength = jnp.exp(-conc_decay * (1.0 - concentration)) * thickness
    covered = ice_mask.astype(jnp.float32)
    moving = covered * land_mask.astype(jnp.float32)
    slope = slope_force(extend(surface[2:3], 1)[0])
    velocity = velocity_start
    stress = jnp.zeros((3, NY, NX), jnp.float32)
    for cycle in range(SUB):
        stress = stresses(extend(velocity, 1), stress, strength, covered)
        velocity = momentum(velocity, extend(stress, 1), thickness, surface[0:2], slope, wind_stress, moving)
    return (velocity, stress)
```

```python
import functools
import math

import jax
import jax.numpy as jnp
from jax import lax
from jax.experimental import pallas as pl
from jax.experimental.pallas import tpu as pltpu
from jax.sharding import PartitionSpec as P

SUB = 4
HALO = 8
CHUNKS = 4
PLAIN = 3
VMEM_OUT = 8 * 1024 * 1024
LANES = 128
MESH = pl.DeviceIdType.MESH

U, V, WX, WY, MASS, GRIP = range(6)
FIELDS = 6


def chunk_order():
    return [0, CHUNKS - 1] + list(range(1, CHUNKS - 1))


def numbered(secs, rows_g):
    order = chunk_order()
    others, cross = range(1, secs), range(2, rows_g)
    sends, gets = {}, {}
    for q in order:
        for i in others:
            for t in [0] + ([1] if q in order[:PLAIN] else []) + list(cross):
                sends["y", i, t, q] = len(sends)
                gets["y", i, t, q] = len(gets)
            if q in order[PLAIN:]:
                sends["a", i, q] = len(sends)
                gets["a", i, q] = len(gets)
        sends["p", q] = len(sends)
        gets["p", q] = len(gets)
        for t in cross:
            sends["c", t, q] = len(sends)
            gets["x", t, q] = len(gets)
        for m in range(1, rows_g // 2):
            gets["z", m, q] = len(gets)
    return sends, gets


def kernel(
    dims,
    weight_hbm,
    ocean_hbm,
    vel_hbm,
    wind_hbm,
    thick_hbm,
    conc_hbm,
    ice_hbm,
    land_hbm,
    fields,
    stress,
    ocean,
    send_codes,
    send_scales,
    recv_codes,
    recv_scales,
    vel_in,
    wind_in,
    thick_in,
    conc_in,
    ice_in,
    land_in,
    surf,
    ns_field_send,
    ns_field,
    ew_send,
    ew_recv,
    ns_surf_send,
    ns_surf,
    side_send,
    side_recv,
    edge_send,
    edge_recv,
    weight_ref,
    weight_sem,
    first_sems,
    ocean_sems,
    static_sems,
    send_sems,
    recv_sems,
    ns_sems,
    ew_sems,
    surf_sems,
    side_sends_sem,
    side_sems,
    edge_sems,
    gate,
):
    secs, rows_g, cols_g, levels = dims
    held = ocean_hbm.shape[0]
    tile_rows, tile_cols = thick_hbm.shape
    tiles = tile_cols // LANES
    top = 2 * HALO
    end = top + tile_rows
    size = tile_rows // CHUNKS
    pairs = rows_g // 2
    s, g, x = lax.axis_index("sec"), lax.axis_index("gy"), lax.axis_index("gx")
    ranks = secs * rows_g
    rank = s * rows_g + g
    pair = g // 2
    odd = lax.rem(g, 2)

    def at_rank(number):
        number = lax.rem(number + ranks, ranks)
        return (number // rows_g, lax.rem(number, rows_g), x)

    def row_of(t):
        if t == 0:
            return g
        if t == 1:
            return g + 1 - 2 * odd
        return 2 * lax.rem(pair + t // 2, pairs) + t % 2

    north, south = at_rank(rank - 1), at_rank(rank + 1)
    west = (s, g, lax.rem(x + cols_g - 1, cols_g))
    east = (s, g, lax.rem(x + 1, cols_g))
    over_secs = [(lax.rem(s + i, secs), g, x) for i in range(1, secs)]
    mate = (s, row_of(1), x)
    others = range(1, secs)
    cross = range(2, rows_g)
    order = chunk_order()
    traded = order[PLAIN:]
    sends, gets = numbered(secs, rows_g)

    weight_copy = pltpu.make_async_copy(weight_hbm, weight_ref, weight_sem)
    weight_copy.start()
    reads = {}

    def read(key, i, t, first, count, sem):
        block = lax.rem(s + i, secs) * rows_g + row_of(t)
        at = pl.ds(pl.multiple_of(block * tile_rows + first, 16), count)
        copy = pltpu.make_async_copy(
            ocean_hbm.at[:, :, at, :],
            ocean.at[i * rows_g + t, :, :, pl.ds(first, count), :],
            sem,
        )
        copy.start()
        reads[key] = copy

    def read_whole(i, t):
        read((i, t), i, t, 0, tile_rows, ocean_sems.at[i * rows_g + t])

    for i in others:
        for t in cross:
            read((i, t, 0), i, t, 0, size, first_sems.at[i - 1, t - 2])

    def greet(semaphore, devices):
        for device in devices + over_secs:
            pl.semaphore_signal(semaphore, inc=1, device_id=device, device_id_type=MESH)

        @pl.when(g > 0)
        def _():
            above = (s, g - 1, x)
            pl.semaphore_signal(semaphore, inc=1, device_id=above, device_id_type=MESH)

        @pl.when(g < rows_g - 1)
        def _():
            below = (s, g + 1, x)
            pl.semaphore_signal(semaphore, inc=1, device_id=below, device_id_type=MESH)

    in_line = jnp.where(g > 0, 1, 0) + jnp.where(g < rows_g - 1, 1, 0)
    barrier = pltpu.get_barrier_semaphore()
    greet(barrier, [west, east])
    weight_copy.wait()
    own_weights = [weight_ref[rank * held + k] for k in range(held)]
    strips = size // 16

    def need(i, t, q):
        key = (i, t, 0) if q == 0 and (i, t, 0) in firsts else (i, t)
        if key in reads:
            reads.pop(key).wait()

    firsts = set(reads)
    static_copies = []

    def read_rest():
        for i in others:
            for t in cross:
                read((i, t), i, t, size, tile_rows - size, ocean_sems.at[i * rows_g + t])
        for i in others:
            read_whole(i, 1)
        read_whole(0, 1)
        for i in others:
            read_whole(i, 0)
        for t in cross:
            read_whole(0, t)
        for n, (source, target) in enumerate(
            (
                (vel_hbm, vel_in),
                (wind_hbm, wind_in),
                (thick_hbm, thick_in),
                (conc_hbm, conc_in),
                (ice_hbm, ice_in),
                (land_hbm, land_in),
            )
        ):
            copy = pltpu.make_async_copy(source, target, static_sems.at[n])
            copy.start()
            static_copies.append(copy)
        read_whole(0, 0)

    def remote(source, target, send_sem, recv_sem, device):
        return pltpu.make_async_remote_copy(
            src_ref=source,
            dst_ref=target,
            send_sem=send_sem,
            recv_sem=recv_sem,
            device_id=device,
            device_id_type=MESH,
        )

    def message(send, get, device):
        return (
            remote(
                send_codes.at[send], recv_codes.at[get], send_sems.at[0], recv_sems.at[get, 0], device
            ),
            remote(
                send_scales.at[send], recv_scales.at[get], send_sems.at[1], recv_sems.at[get, 1], device
            ),
        )

    def start(copies):
        for copy in copies:
            copy.start()

    def arrived(get):
        for copy in message(0, get, mate):
            copy.wait_recv()
        return recv_codes.at[get], recv_scales.at[get]

    def level_sum(i, t, q, c, at, j):
        rows = pl.ds(q * size + at.start, 16)
        cols = pl.ds(j * LANES, LANES)
        slot = i * rows_g + t
        value = own_weights[0] * ocean[slot, 0, c, rows, cols].astype(jnp.float32)
        for k in range(1, held):
            value = value + own_weights[k] * ocean[slot, k, c, rows, cols].astype(jnp.float32)
        return value

    def decoded(codes, scale, c, at, j):
        code = codes[c, at, pl.ds(j * LANES, LANES)].astype(jnp.int32)
        return code.astype(jnp.float32) * scale

    def summed(i, t, q, received):
        def parts(c):
            scales = [scale[pl.ds(c, 1), :] for _, scale in received]

            def value_of(at, j):
                value = level_sum(i, t, q, c, at, j)
                for (codes, _), scale in zip(received, scales):
                    value = value + decoded(codes, scale, c, at, j)
                return value

            return value_of

        return parts

    def coded(parts, send):
        for c in range(3):
            value_of = parts(c)
            values = {}
            most = None
            for n in range(strips):
                at = pl.ds(n * 16, 16)
                for j in range(tiles):
                    value = value_of(at, j)
                    values[n, j] = value
                    size_of = jnp.abs(value)
                    most = size_of if most is None else jnp.maximum(most, size_of)
            most = jnp.maximum(jnp.max(most, axis=0, keepdims=True), 1e-30)
            send_scales[send, pl.ds(c, 1), :] = most * (1.0 / 32767.0)
            inverse = 32767.0 / most
            for (n, j), value in values.items():
                code = jnp.round(value * inverse)
                send_codes[send, c, pl.ds(n * 16, 16), pl.ds(j * LANES, LANES)] = code.astype(
                    jnp.int32
                ).astype(jnp.int16)

    def send_y(i, t, q, received):
        need(i, t, q)
        coded(summed(i, t, q, received), sends["y", i, t, q])

    def start_y(i, t, q):
        start(message(sends["y", i, t, q], gets["y", i, t, q], over_secs[i - 1]))

    def send_p(q):
        need(0, 1, q)
        received = []
        if q not in traded:
            received = [arrived(gets["y", i, 1, q]) for i in others]
        coded(summed(0, 1, q, received), sends["p", q])
        start(message(sends["p", q], gets["p", q], mate))

    def send_a(q):
        for i in others:
            need(i, 1, q)
            coded(summed(i, 1, q, []), sends["a", i, q])
            start(message(sends["a", i, q], gets["a", i, q], mate))

    floods = rows_g - 1
    flooded = 0

    def flood_to(number):
        nonlocal flooded
        while flooded < number:
            pl.semaphore_wait(gate.at[flooded], secs - 1 + in_line)
            flooded += 1
            if flooded < floods:
                greet(gate.at[flooded], [])

    plan = []
    for n, q in enumerate(order):
        plan.append([(t, q) for t in cross])
        if n:
            plan.append([(t, order[n - 1]) for t in (1, 0) if order[n - 1] not in traded])
    plan.append([(t, order[-1]) for t in (1, 0) if order[-1] not in traded])
    begun = False
    for n, group in enumerate(plan):
        if n:
            flood_to(min(n, floods))
        if n == 2:
            for q in traded:
                send_a(q)
            for q in traded:
                send_p(q)
        for t, q in group:
            for i in others:
                send_y(i, t, q, [])
                if not begun:
                    read_rest()
                    pl.semaphore_wait(barrier, secs + 1 + in_line)
                start_y(i, t, q)
                if not begun:
                    greet(gate.at[0], [])
                    begun = True
    flood_to(floods)

    has_north, has_south = rank > 0, rank < ranks - 1

    def rows_up(source, target, sems):
        return remote(
            source.at[0], target.at[1], sems.at[0, 0], sems.at[0, 1], north
        )

    def rows_down(source, target, sems):
        return remote(
            source.at[1],
            target.at[0],
            sems.at[1, 0],
            sems.at[1, 1],
            south,
        )

    def either(condition, yes, no):
        pl.when(condition)(yes)
        pl.when(jnp.logical_not(condition))(no)

    def place_rows(target, received, count, side, has, waits):
        to = pl.ds(end, HALO) if side else pl.ds(HALO, HALO)

        def there():
            waits()
            for f in range(count):
                for j in range(tiles):
                    target[f, j, to, :] = received[side, f, j]

        def missing():
            for f in range(count):
                for j in range(tiles):
                    target[f, j, to, :] = jnp.zeros((HALO, LANES), jnp.float32)

        either(has, there, missing)

    lane = lax.broadcasted_iota(jnp.int32, (8, LANES), 1)
    all_strips = (tile_rows + 2 * HALO) // 8

    def beyond(west_value, east_value):
        return jnp.where(
            lane < HALO, east_value, jnp.where(lane >= LANES - HALO, west_value, 0.0)
        )

    per_piece = LANES // HALO

    def edges_of(ref, places):
        out = []
        for j, offset in ((0, 0), (tiles - 1, HALO)):
            packed = [jnp.zeros((8, LANES), jnp.float32)] * pl.cdiv(len(places), per_piece)
            for n, (c, row) in enumerate(places):
                piece, spot = divmod(n, per_piece)
                value = ref[c, j, pl.ds(row, 8), :]
                shift = (spot * HALO + offset) % LANES
                value = pltpu.roll(value, shift, 1) if shift else value
                packed[piece] = jnp.where(lane // HALO == spot, value, packed[piece])
            out.append(packed)
        return out

    def place_edges(ref, places, west_values, east_values):
        for n, (c, row) in enumerate(places):
            piece, spot = divmod(n, per_piece)
            back = (LANES - HALO - spot * HALO) % LANES
            from_west = west_values[piece]
            from_west = pltpu.roll(from_west, back, 1) if back else from_west
            back = (LANES - spot * HALO) % LANES
            from_east = east_values[piece]
            from_east = pltpu.roll(from_east, back, 1) if back else from_east
            ref[c, tiles, pl.ds(row, 8), :] = beyond(from_west, from_east)

    def sideways(sends, gets, sems):
        return (
            remote(sends.at[0], gets.at[1], sems.at[0, 0], sems.at[0, 1], west),
            remote(sends.at[1], gets.at[0], sems.at[1, 0], sems.at[1, 1], east),
        )

    field_columns = sideways(ew_send, ew_recv, ew_sems)
    field_places = [(f, HALO + 8 * n) for f in range(FIELDS) for n in range(all_strips)]
    field_pieces = range(ew_recv.shape[1])
    every = tiles + 1
    relay = {t: (row_of(t) > g) == (odd == 1) for t in cross}

    def cross_message(t, q, relaying):
        @pl.when(relay[t] if relaying else jnp.logical_not(relay[t]))
        def _():
            received = [arrived(gets["y", i, t, q]) for i in others]
            send = sends["c", t, q]
            if relaying:
                received.append(arrived(gets["x", t, q]))
            coded(summed(0, t, q, received), send)
            if relaying:
                start(message(send, gets["z", t // 2, q], (s, row_of(t), x)))
            else:
                start(message(send, gets["x", t, q], mate))

    def statics():
        for copy in static_copies:
            copy.wait()

        @pl.loop(0, tile_rows // 8)
        def _(i):
            at = pl.ds(pl.multiple_of(i * 8, 8), 8)
            to = pl.ds(pl.multiple_of(i * 8 + top, 8), 8)
            for j in range(tiles):
                cols = pl.ds(j * LANES, LANES)
                for f in range(2):
                    fields[U + f, j, to, :] = vel_in[f, at, cols]
                    fields[WX + f, j, to, :] = wind_in[f, at, cols]
                thick = thick_in[at, cols]
                ice = ice_in[at, cols].astype(jnp.float32)
                strength = jnp.exp(-4.0 * (1.0 - conc_in[at, cols])) * thick
                fields[GRIP, j, to, :] = strength * ice * (1.0 / 3.0)
                fields[MASS, j, to, :] = thick * (ice * land_in[at, cols].astype(jnp.float32))

        for f in range(FIELDS):
            for j in range(tiles):
                ns_field_send[0, f, j] = fields[f, j, pl.ds(top, HALO), :]
                ns_field_send[1, f, j] = fields[f, j, pl.ds(end - HALO, HALO), :]

        @pl.when(has_north)
        def _():
            rows_up(ns_field_send, ns_field, ns_sems).start()

        @pl.when(has_south)
        def _():
            rows_down(ns_field_send, ns_field, ns_sems).start()

    def field_halo():
        place_rows(
            fields, ns_field, FIELDS, 0, has_north,
            lambda: rows_down(ns_field_send, ns_field, ns_sems).wait_recv(),
        )
        place_rows(
            fields, ns_field, FIELDS, 1, has_south,
            lambda: rows_up(ns_field_send, ns_field, ns_sems).wait_recv(),
        )

        @pl.when(has_north)
        def _():
            rows_up(ns_field_send, ns_field, ns_sems).wait_send()

        @pl.when(has_south)
        def _():
            rows_down(ns_field_send, ns_field, ns_sems).wait_send()

        for side, packed in enumerate(edges_of(fields, field_places)):
            for piece, value in enumerate(packed):
                ew_send[side, piece] = value
        start(field_columns)

    def margins(target, count):
        zero = jnp.zeros((8, LANES), jnp.float32)
        for f in range(count):
            for j in range(every):
                target[f, j, pl.ds(0, HALO), :] = zero
                target[f, j, pl.ds(end + HALO, HALO), :] = zero

    def sides(values):
        before = [pltpu.roll(value, 1, 1) for value in values]
        after = [pltpu.roll(value, LANES - 1, 1) for value in values]
        out = []
        for j in range(every):
            low = jnp.where(lane == 0, before[j - 1], before[j])
            high = jnp.where(lane == LANES - 1, after[(j + 1) % every], after[j])
            out.append(0.5 * (high - low))
        return out

    def strip_rows(i, shift):
        if shift == 0:
            return pl.ds(pl.multiple_of(i * 8 + HALO, 8), 8)
        return pl.ds(i * 8 + HALO + shift, 8)

    def rows_of(ref, f, at):
        return [ref[f, j, at, :] for j in range(every)]

    def stress_step(first):
        @pl.loop(0, all_strips, unroll=True)
        def _(i):
            at, up, down = strip_rows(i, 0), strip_rows(i, -1), strip_rows(i, 1)
            east_u = sides(rows_of(fields, U, at))
            east_v = sides(rows_of(fields, V, at))
            for j in range(every):
                north_u = 0.5 * (fields[U, j, down, :] - fields[U, j, up, :])
                north_v = 0.5 * (fields[V, j, down, :] - fields[V, j, up, :])
                spread = east_u[j] + north_v
                tension = east_u[j] - north_v
                shear = north_u + east_v[j]
                turned = lax.rsqrt(
                    spread * spread + 0.25 * (tension * tension + shear * shear) + 0.01
                )
                grip = fields[GRIP, j, at, :]
                rate = grip * turned
                new0 = rate * spread - grip
                new1 = (0.25 * rate) * tension
                new2 = (0.125 * rate) * shear
                if not first:
                    new0 = stress[0, j, at, :] * (1.0 / 1.5) + new0
                    new1 = stress[1, j, at, :] * (1.0 / 1.5) + new1
                    new2 = stress[2, j, at, :] * (1.0 / 1.5) + new2
                stress[0, j, at, :] = new0
                stress[1, j, at, :] = new1
                stress[2, j, at, :] = new2

    def velocity_step(first_strip=0, last_strip=all_strips, width=tiles + 1):
        @pl.loop(first_strip, last_strip, unroll=True)
        def _(i):
            at, up, down = strip_rows(i, 0), strip_rows(i, -1), strip_rows(i, 1)
            first = rows_of(stress, 0, at)
            second = rows_of(stress, 1, at)
            east_normal = sides([0.5 * (a + b) for a, b in zip(first, second)])
            east_third = sides(rows_of(stress, 2, at))
            for j in range(width):
                north_third = 0.5 * (stress[2, j, down, :] - stress[2, j, up, :])
                north_normal = 0.25 * (
                    (stress[0, j, down, :] - stress[1, j, down, :])
                    - (stress[0, j, up, :] - stress[1, j, up, :])
                )
                u, v = fields[U, j, at, :], fields[V, j, at, :]
                cx, cy = surf[0, j, at, :], surf[1, j, at, :]
                mass = fields[MASS, j, at, :]
                rel_u, rel_v = cx - u, cy - v
                drag = 0.8 * jnp.sqrt(rel_u * rel_u + rel_v * rel_v)
                a = mass + drag
                b = 0.5 * mass
                rx = mass * u + (east_normal[j] + north_third) + drag * cx + fields[WX, j, at, :]
                ry = mass * v + (east_third[j] + north_normal) + drag * cy + fields[WY, j, at, :]
                live = mass > 0.0
                inverse = 1.0 / jnp.where(live, a * a + b * b, 1.0)
                fields[U, j, at, :] = jnp.where(live, (a * rx + b * ry) * inverse, 0.0)
                fields[V, j, at, :] = jnp.where(live, (a * ry - b * rx) * inverse, 0.0)

    def first_stress():
        for copy in field_columns:
            copy.wait()
        place_edges(
            fields,
            field_places,
            [ew_recv[0, piece] for piece in field_pieces],
            [ew_recv[1, piece] for piece in field_pieces],
        )
        margins(fields, 2)
        margins(stress, 3)
        margins(surf, 3)
        stress_step(True)

    norm = 1.0 / math.sqrt(levels)
    chunk_strips = size // 8
    pieces = side_send.shape[2]
    first_rows, last_rows = pl.ds(top, HALO), pl.ds(end - HALO, HALO)

    def up_halo():
        return remote(
            ns_surf_send.at[0], ns_surf.at[1], surf_sems.at[0, 0], surf_sems.at[0, 1], north
        )

    def down_halo():
        return remote(
            ns_surf_send.at[1], ns_surf.at[0], surf_sems.at[1, 0], surf_sems.at[1, 1], south
        )

    def inside(q):
        return [(c, top + q * size + 8 * n) for c in range(3) for n in range(chunk_strips)]

    outside = [(c, row) for c in range(3) for row in (HALO, end)]

    def side_copies(q):
        return (
            remote(side_send.at[q, 0], side_recv.at[q, 1], side_sends_sem, side_sems.at[q, 1], west),
            remote(side_send.at[q, 1], side_recv.at[q, 0], side_sends_sem, side_sems.at[q, 0], east),
        )

    def surface(q):
        need(0, 0, q)
        received = [arrived(gets["y", i, 0, q]) for i in others]
        received.append(arrived(gets["p", q]))
        received += [arrived(gets["z", m, q]) for m in range(1, pairs)]
        parts = summed(0, 0, q, received)
        for c in range(3):
            value_of = parts(c)
            for n in range(strips):
                for j in range(tiles):
                    to = pl.ds(top + q * size + n * 16, 16)
                    surf[c, j, to, :] = value_of(pl.ds(n * 16, 16), j) * norm
        for side, packed in enumerate(edges_of(surf, inside(q))):
            for piece in range(pieces):
                side_send[q, side, piece] = packed[piece]
        start(side_copies(q))
        for side, edge, rows in ((0, 0, first_rows), (1, CHUNKS - 1, last_rows)):
            if q == edge:
                for c in range(3):
                    for j in range(tiles):
                        ns_surf_send[side, c, j] = surf[c, j, rows, :]
        if q == 0:

            @pl.when(has_north)
            def _():
                up_halo().start()

        if q == CHUNKS - 1:

            @pl.when(has_south)
            def _():
                down_halo().start()

    def place_halo(side, has, wait):
        to = pl.ds(end, HALO) if side else pl.ds(HALO, HALO)

        def there():
            wait()
            for c in range(3):
                for j in range(tiles):
                    surf[c, j, to, :] = ns_surf[side, c, j]

        def missing():
            for c in range(3):
                for j in range(tiles):
                    surf[c, j, to, :] = jnp.zeros((HALO, LANES), jnp.float32)

        either(has, there, missing)

    edge_copies = sideways(edge_send, edge_recv, edge_sems)

    def surface_halo():
        place_halo(0, has_north, lambda: down_halo().wait_recv())
        place_halo(1, has_south, lambda: up_halo().wait_recv())

        @pl.when(has_north)
        def _():
            up_halo().wait_send()

        @pl.when(has_south)
        def _():
            down_halo().wait_send()

        for side, packed in enumerate(edges_of(surf, outside)):
            edge_send[side] = packed[0]
        start(edge_copies)

    def surface_sides(q):
        for copy in side_copies(q):
            copy.wait_recv()
        place_edges(
            surf,
            inside(q),
            [side_recv[q, 0, piece] for piece in range(pieces)],
            [side_recv[q, 1, piece] for piece in range(pieces)],
        )

    for n, q in enumerate(order):
        for t in cross:
            need(0, t, q)
            cross_message(t, q, False)
        if n and order[n - 1] not in traded:
            send_p(order[n - 1])
        for t in cross:
            cross_message(t, q, True)
        if n == 0:
            statics()
            for late in traded:
                for i in others:
                    send_y(i, 0, late, [arrived(gets["a", i, late])])
                    start_y(i, 0, late)
        if n == 2:
            field_halo()
        if n >= 2:
            surface(order[n - 2])
    if order[-1] not in traded:
        send_p(order[-1])
    first_stress()
    surface(order[-2])
    for q in order[:-2]:
        surface_sides(q)
    surface_halo()
    surface_sides(order[-2])
    for send_sem, source in ((send_sems.at[0], send_codes), (send_sems.at[1], send_scales)):
        remote(source, source, send_sem, recv_sems.at[0, 0], mate).wait_send()
    surface(order[-1])
    for copy in edge_copies:
        copy.wait()
    place_edges(surf, outside, [edge_recv[0]], [edge_recv[1]])
    surface_sides(order[-1])
    remote(side_send, side_recv, side_sends_sem, side_sems.at[0, 0], west).wait_send()

    @pl.loop(0, all_strips, unroll=True)
    def _(i):
        at, up, down = strip_rows(i, 0), strip_rows(i, -1), strip_rows(i, 1)
        slope_x = sides(rows_of(surf, 2, at))
        for j in range(every):
            slope_y = 0.5 * (surf[2, j, down, :] - surf[2, j, up, :])
            gain = -0.5 * fields[MASS, j, at, :]
            fields[WX, j, at, :] = fields[WX, j, at, :] + gain * slope_x[j]
            fields[WY, j, at, :] = fields[WY, j, at, :] + gain * slope_y

    velocity_step()

    @pl.loop(0, SUB - 2)
    def _(cycle):
        stress_step(False)
        velocity_step()

    stress_step(False)
    velocity_step(1, all_strips - 1, tiles)

def write_out(fields, stress, vel_out, stress_out, sems):
    tiles = fields.shape[1] - 1
    rows = pl.ds(2 * HALO, vel_out.shape[1])
    copies = []
    for j in range(tiles):
        cols = pl.ds(j * LANES, LANES)
        for n, (source, target) in enumerate(
            ((fields.at[pl.ds(U, 2)], vel_out), (stress, stress_out))
        ):
            copy = pltpu.make_async_copy(
                source.at[:, j, rows, :], target.at[:, :, cols], sems.at[n, j]
            )
            copy.start()
            copies.append(copy)
    for copy in copies:
        copy.wait()


def body(
    ocean, level_weight, velocity_start, wind_stress, thickness, concentration, ice_mask, land_mask
):
    secs, rows_g, cols_g = lax.axis_size("sec"), lax.axis_size("gy"), lax.axis_size("gx")
    held = ocean.shape[0]
    rows, cols = thickness.shape
    tiles = cols // LANES
    tall = rows + 4 * HALO
    wide_rows = rows + 2 * HALO
    size = rows // CHUNKS
    pieces = pl.cdiv(3 * (size // 8), LANES // HALO)
    field_pieces = pl.cdiv(FIELDS * (wide_rows // 8), LANES // HALO)
    f32, i16 = jnp.float32, jnp.int16
    dma = pltpu.SemaphoreType.DMA
    anywhere = pl.BlockSpec(memory_space=pl.ANY)
    on_chip = pl.BlockSpec(memory_space=pltpu.VMEM)
    sends, gets = numbered(secs, rows_g)
    fields, stress = pl.pallas_call(
        functools.partial(kernel, (secs, rows_g, cols_g, level_weight.shape[0])),
        out_shape=(
            pltpu.VMEM((FIELDS, tiles + 1, tall, LANES), f32),
            pltpu.VMEM((3, tiles + 1, tall, LANES), f32),
        ),
        in_specs=[anywhere] * 8,
        out_specs=(on_chip, on_chip),
        scratch_shapes=[
            pltpu.VMEM((secs * rows_g, held, 3, rows, cols), ocean.dtype),
            pltpu.VMEM((len(sends), 3, size, cols), i16),
            pltpu.VMEM((len(sends), 3, LANES), f32),
            pltpu.VMEM((len(gets), 3, size, cols), i16),
            pltpu.VMEM((len(gets), 3, LANES), f32),
            pltpu.VMEM((2, rows, cols), f32),
            pltpu.VMEM((2, rows, cols), f32),
            pltpu.VMEM((rows, cols), f32),
            pltpu.VMEM((rows, cols), f32),
            pltpu.VMEM((rows, cols), jnp.int32),
            pltpu.VMEM((rows, cols), jnp.int32),
            pltpu.VMEM((3, tiles + 1, tall, LANES), f32),
            pltpu.VMEM((2, FIELDS, tiles, HALO, LANES), f32),
            pltpu.VMEM((2, FIELDS, tiles, HALO, LANES), f32),
            pltpu.VMEM((2, field_pieces, 8, LANES), f32),
            pltpu.VMEM((2, field_pieces, 8, LANES), f32),
            pltpu.VMEM((2, 3, tiles, HALO, LANES), f32),
            pltpu.VMEM((2, 3, tiles, HALO, LANES), f32),
            pltpu.VMEM((CHUNKS, 2, pieces, 8, LANES), f32),
            pltpu.VMEM((CHUNKS, 2, pieces, 8, LANES), f32),
            pltpu.VMEM((2, 8, LANES), f32),
            pltpu.VMEM((2, 8, LANES), f32),
            pltpu.SMEM(level_weight.shape, f32),
            dma(()),
            dma((secs - 1, rows_g - 2)),
            dma((secs * rows_g,)),
            dma((6,)),
            dma((2,)),
            dma((len(gets), 2)),
            dma((2, 2)),
            dma((2, 2)),
            dma((2, 2)),
            dma(()),
            dma((CHUNKS, 2)),
            dma((2, 2)),
            pltpu.SemaphoreType.REGULAR((rows_g - 1,)),
        ],
        compiler_params=pltpu.CompilerParams(
            collective_id=0, has_side_effects=True, vmem_limit_bytes=52 * 1024 * 1024
        ),
    )(
        level_weight,
        ocean,
        velocity_start,
        wind_stress,
        thickness,
        concentration,
        ice_mask,
        land_mask,
    )
    return pl.pallas_call(
        write_out,
        out_shape=(
            jax.ShapeDtypeStruct((2, rows, cols), f32),
            jax.ShapeDtypeStruct((3, rows, cols), f32),
        ),
        in_specs=[on_chip, on_chip],
        out_specs=(anywhere, anywhere),
        scratch_shapes=[dma((2, tiles))],
        compiler_params=pltpu.CompilerParams(vmem_limit_bytes=VMEM_OUT),
    )(fields, stress)


def solution(mesh):
    placed = (
        P(("sec", "gy"), None, None, "gx"),
        P(),
        P(None, ("sec", "gy"), "gx"),
        P(None, ("sec", "gy"), "gx"),
        P(("sec", "gy"), "gx"),
        P(("sec", "gy"), "gx"),
        P(("sec", "gy"), "gx"),
        P(("sec", "gy"), "gx"),
    )
    return jax.shard_map(
        body,
        mesh=mesh,
        in_specs=placed,
        out_specs=(P(None, ("sec", "gy"), "gx"), P(None, ("sec", "gy"), "gx")),
        check_vma=False,
    )
```

```python
import functools
import math

import jax
import jax.numpy as jnp
from jax import lax
from jax.experimental import pallas as pl
from jax.experimental.pallas import tpu as pltpu
from jax.sharding import PartitionSpec as P

SUB = 4
HALO = 8
CHUNKS = 4
PLAIN = 3
LEAD = 2
VMEM_OUT = 8 * 1024 * 1024
LANES = 128
MESH = pl.DeviceIdType.MESH

U, V, WX, WY, MASS, GRIP = range(6)
FIELDS = 6


def chunk_order():
    return [0, CHUNKS - 1] + list(range(1, CHUNKS - 1))


def numbered(secs, rows_g):
    order = chunk_order()
    others, cross = range(1, secs), range(2, rows_g)
    sends, gets = {}, {}
    for q in order:
        for i in others:
            for t in [0] + ([1] if q in order[:PLAIN] else []) + list(cross):
                sends["y", i, t, q] = len(sends)
                gets["y", i, t, q] = len(gets)
            if q in order[PLAIN:]:
                sends["a", i, q] = len(sends)
                gets["a", i, q] = len(gets)
        sends["p", q] = len(sends)
        gets["p", q] = len(gets)
        for t in cross:
            sends["c", t, q] = len(sends)
            gets["x", t, q] = len(gets)
        for m in range(1, rows_g // 2):
            gets["z", m, q] = len(gets)
    return sends, gets


def kernel(
    dims,
    weight_hbm,
    ocean_hbm,
    vel_hbm,
    wind_hbm,
    thick_hbm,
    conc_hbm,
    ice_hbm,
    land_hbm,
    fields,
    stress,
    ocean,
    send_codes,
    send_scales,
    recv_codes,
    recv_scales,
    vel_in,
    wind_in,
    thick_in,
    conc_in,
    ice_in,
    land_in,
    surf,
    ns_codes,
    ns_scales,
    ns_got,
    ns_scales_got,
    ew_send,
    ew_recv,
    ns_surf_send,
    ns_surf,
    side_send,
    side_recv,
    corner_recv,
    weight_ref,
    weight_sem,
    first_sems,
    ocean_sems,
    static_sems,
    send_sems,
    recv_sems,
    ns_sems,
    ew_sems,
    surf_sems,
    side_sends_sem,
    side_sems,
    gate,
):
    secs, rows_g, cols_g, levels = dims
    held = ocean_hbm.shape[0]
    tile_rows, tile_cols = thick_hbm.shape
    tiles = tile_cols // LANES
    top = 2 * HALO
    end = top + tile_rows
    size = tile_rows // CHUNKS
    pairs = rows_g // 2
    s, g, x = lax.axis_index("sec"), lax.axis_index("gy"), lax.axis_index("gx")
    ranks = secs * rows_g
    rank = s * rows_g + g
    pair = g // 2
    odd = lax.rem(g, 2)

    def at_rank(number):
        number = lax.rem(number + ranks, ranks)
        return (number // rows_g, lax.rem(number, rows_g), x)

    def row_of(t):
        if t == 0:
            return g
        if t == 1:
            return g + 1 - 2 * odd
        return 2 * lax.rem(pair + t // 2, pairs) + t % 2

    north, south = at_rank(rank - 1), at_rank(rank + 1)
    west = (s, g, lax.rem(x + cols_g - 1, cols_g))
    east = (s, g, lax.rem(x + 1, cols_g))
    north_west, north_east = north[:2] + west[2:], north[:2] + east[2:]
    south_west, south_east = south[:2] + west[2:], south[:2] + east[2:]
    over_secs = [(lax.rem(s + i, secs), g, x) for i in range(1, secs)]
    mate = (s, row_of(1), x)
    others = range(1, secs)
    cross = range(2, rows_g)
    order = chunk_order()
    traded = order[PLAIN:]
    sends, gets = numbered(secs, rows_g)

    weight_copy = pltpu.make_async_copy(weight_hbm, weight_ref, weight_sem)
    weight_copy.start()
    reads = {}

    def read(key, i, t, first, count, sem):
        block = lax.rem(s + i, secs) * rows_g + row_of(t)
        at = pl.ds(pl.multiple_of(block * tile_rows + first, 16), count)
        copy = pltpu.make_async_copy(
            ocean_hbm.at[:, :, at, :],
            ocean.at[i * rows_g + t, :, :, pl.ds(first, count), :],
            sem,
        )
        copy.start()
        reads[key] = copy

    def read_whole(i, t):
        read((i, t), i, t, 0, tile_rows, ocean_sems.at[i * rows_g + t])

    for i in others:
        for t in cross:
            read((i, t, 0), i, t, 0, size, first_sems.at[i - 1, t - 2])

    def greet(semaphore, devices):
        for device in devices + over_secs:
            pl.semaphore_signal(semaphore, inc=1, device_id=device, device_id_type=MESH)

        @pl.when(g > 0)
        def _():
            above = (s, g - 1, x)
            pl.semaphore_signal(semaphore, inc=1, device_id=above, device_id_type=MESH)

        @pl.when(g < rows_g - 1)
        def _():
            below = (s, g + 1, x)
            pl.semaphore_signal(semaphore, inc=1, device_id=below, device_id_type=MESH)

    in_line = jnp.where(g > 0, 1, 0) + jnp.where(g < rows_g - 1, 1, 0)
    barrier = pltpu.get_barrier_semaphore()
    greet(barrier, [west, east])
    weight_copy.wait()
    own_weights = [weight_ref[rank * held + k] for k in range(held)]
    strips = size // 16

    def need(i, t, q):
        key = (i, t, 0) if q == 0 and (i, t, 0) in firsts else (i, t)
        if key in reads:
            reads.pop(key).wait()

    firsts = set(reads)
    static_copies = []

    def read_rest():
        for i in others:
            for t in cross:
                read((i, t), i, t, size, tile_rows - size, ocean_sems.at[i * rows_g + t])
        for i in others:
            read_whole(i, 1)
        read_whole(0, 1)
        for i in others:
            read_whole(i, 0)
        for t in cross:
            read_whole(0, t)
        for n, (source, target) in enumerate(
            (
                (vel_hbm, vel_in),
                (wind_hbm, wind_in),
                (thick_hbm, thick_in),
                (conc_hbm, conc_in),
                (ice_hbm, ice_in),
                (land_hbm, land_in),
            )
        ):
            copy = pltpu.make_async_copy(source, target, static_sems.at[n])
            copy.start()
            static_copies.append(copy)
        read_whole(0, 0)

    def remote(source, target, send_sem, recv_sem, device):
        return pltpu.make_async_remote_copy(
            src_ref=source,
            dst_ref=target,
            send_sem=send_sem,
            recv_sem=recv_sem,
            device_id=device,
            device_id_type=MESH,
        )

    def message(send, get, device):
        return (
            remote(
                send_codes.at[send], recv_codes.at[get], send_sems.at[0], recv_sems.at[get, 0], device
            ),
            remote(
                send_scales.at[send], recv_scales.at[get], send_sems.at[1], recv_sems.at[get, 1], device
            ),
        )

    def start(copies):
        for copy in copies:
            copy.start()

    def arrived(get):
        for copy in message(0, get, mate):
            copy.wait_recv()
        return recv_codes.at[get], recv_scales.at[get]

    def level_sum(i, t, q, c, at, j):
        rows = pl.ds(q * size + at.start, 16)
        cols = pl.ds(j * LANES, LANES)
        slot = i * rows_g + t
        value = own_weights[0] * ocean[slot, 0, c, rows, cols].astype(jnp.float32)
        for k in range(1, held):
            value = value + own_weights[k] * ocean[slot, k, c, rows, cols].astype(jnp.float32)
        return value

    def decoded(codes, scale, c, at, j):
        code = codes[c, at, pl.ds(j * LANES, LANES)].astype(jnp.int32)
        return code.astype(jnp.float32) * scale

    def summed(i, t, q, received):
        def parts(c):
            scales = [scale[pl.ds(c, 1), :] for _, scale in received]

            def value_of(at, j):
                value = level_sum(i, t, q, c, at, j)
                for (codes, _), scale in zip(received, scales):
                    value = value + decoded(codes, scale, c, at, j)
                return value

            return value_of

        return parts

    def coded(parts, send):
        for c in range(3):
            value_of = parts(c)
            values = {}
            most = None
            for n in range(strips):
                at = pl.ds(n * 16, 16)
                for j in range(tiles):
                    value = value_of(at, j)
                    values[n, j] = value
                    size_of = jnp.abs(value)
                    most = size_of if most is None else jnp.maximum(most, size_of)
            most = jnp.maximum(jnp.max(most, axis=0, keepdims=True), 1e-30)
            send_scales[send, pl.ds(c, 1), :] = most * (1.0 / 32767.0)
            inverse = 32767.0 / most
            for (n, j), value in values.items():
                code = jnp.round(value * inverse)
                send_codes[send, c, pl.ds(n * 16, 16), pl.ds(j * LANES, LANES)] = code.astype(
                    jnp.int32
                ).astype(jnp.int16)

    def send_y(i, t, q, received):
        need(i, t, q)
        coded(summed(i, t, q, received), sends["y", i, t, q])

    def start_y(i, t, q):
        start(message(sends["y", i, t, q], gets["y", i, t, q], over_secs[i - 1]))

    def send_p(q):
        need(0, 1, q)
        received = []
        if q not in traded:
            received = [arrived(gets["y", i, 1, q]) for i in others]
        coded(summed(0, 1, q, received), sends["p", q])
        start(message(sends["p", q], gets["p", q], mate))

    def send_a(q):
        for i in others:
            need(i, 1, q)
            coded(summed(i, 1, q, []), sends["a", i, q])
            start(message(sends["a", i, q], gets["a", i, q], mate))

    floods = rows_g
    flooded = 0

    def flood_to(number):
        nonlocal flooded
        while flooded < number:
            pl.semaphore_wait(gate.at[flooded], secs + 1 + in_line)
            flooded += 1
            if flooded < floods:
                greet(gate.at[flooded], [west, east])

    plan = [[(t, q) for t in cross] for q in order[:LEAD]]
    for n, q in enumerate(order):
        if n + LEAD < len(order):
            plan.append([(1, q)] * (q not in traded))
            plan.append([(t, order[n + LEAD]) for t in cross])
            plan.append([(0, q)] * (q not in traded))
        else:
            plan.append([(t, q) for t in (1, 0)] * (q not in traded))
    begun = False
    for n, group in enumerate(plan):
        if n:
            flood_to(min(n, floods))
        if n == 2:
            for q in traded:
                send_a(q)
            for q in traded:
                send_p(q)
        for t, q in group:
            for i in others:
                send_y(i, t, q, [])
                if not begun:
                    read_rest()
                    pl.semaphore_wait(barrier, secs + 1 + in_line)
                start_y(i, t, q)
                if not begun:
                    greet(gate.at[0], [west, east])
                    begun = True
    flood_to(floods)

    has_north, has_south = rank > 0, rank < ranks - 1

    def rows_up():
        return (
            remote(ns_codes.at[0], ns_got.at[1], ns_sems.at[0, 0, 0], ns_sems.at[0, 0, 1], north),
            remote(ns_scales.at[0], ns_scales_got.at[1], ns_sems.at[0, 1, 0], ns_sems.at[0, 1, 1], north),
        )

    def rows_down():
        return (
            remote(ns_codes.at[1], ns_got.at[0], ns_sems.at[1, 0, 0], ns_sems.at[1, 0, 1], south),
            remote(ns_scales.at[1], ns_scales_got.at[0], ns_sems.at[1, 1, 0], ns_sems.at[1, 1, 1], south),
        )

    def pack_rows(side):
        rows = pl.ds(end - HALO, HALO) if side else pl.ds(top, HALO)
        for f in range(0, FIELDS, 2):
            inverses = []
            for k in (f, f + 1):
                most = jnp.abs(fields[k, 0, rows, :])
                for j in range(1, tiles):
                    most = jnp.maximum(most, jnp.abs(fields[k, j, rows, :]))
                most = jnp.maximum(jnp.max(most, axis=0, keepdims=True), 1e-30)
                ns_scales[side, pl.ds(k, 1), :] = most * (1.0 / 32767.0)
                inverses.append(jnp.broadcast_to(32767.0 / most, (HALO, LANES)))
            inverse = jnp.concatenate(inverses, axis=0)
            for j in range(tiles):
                value = jnp.concatenate([fields[f, j, rows, :], fields[f + 1, j, rows, :]], axis=0)
                code = jnp.round(value * inverse).astype(jnp.int32).astype(jnp.int16)
                ns_codes[side, pl.ds(f * HALO, 2 * HALO), pl.ds(j * LANES, LANES)] = code

    def either(condition, yes, no):
        pl.when(condition)(yes)
        pl.when(jnp.logical_not(condition))(no)

    def place_rows(side, has, copies):
        to = pl.ds(end, HALO) if side else pl.ds(HALO, HALO)

        def there():
            for copy in copies():
                copy.wait_recv()
            for f in range(0, FIELDS, 2):
                scales = [ns_scales_got[side, pl.ds(k, 1), :] for k in (f, f + 1)]
                for j in range(tiles):
                    code = ns_got[side, pl.ds(f * HALO, 2 * HALO), pl.ds(j * LANES, LANES)]
                    value = code.astype(jnp.int32).astype(jnp.float32)
                    fields[f, j, to, :] = value[0:HALO] * scales[0]
                    fields[f + 1, j, to, :] = value[HALO : 2 * HALO] * scales[1]

        def missing():
            for f in range(FIELDS):
                for j in range(tiles):
                    fields[f, j, to, :] = jnp.zeros((HALO, LANES), jnp.float32)

        either(has, there, missing)

    lane = lax.broadcasted_iota(jnp.int32, (8, LANES), 1)
    all_strips = (tile_rows + 2 * HALO) // 8

    def beyond(west_value, east_value):
        return jnp.where(
            lane < HALO, east_value, jnp.where(lane >= LANES - HALO, west_value, 0.0)
        )

    per_piece = LANES // HALO

    def edges_of(ref, places):
        out = []
        for j, offset in ((0, 0), (tiles - 1, HALO)):
            packed = [jnp.zeros((8, LANES), jnp.float32)] * pl.cdiv(len(places), per_piece)
            for n, (c, row) in enumerate(places):
                piece, spot = divmod(n, per_piece)
                value = ref[c, j, pl.ds(row, 8), :]
                shift = (spot * HALO + offset) % LANES
                value = pltpu.roll(value, shift, 1) if shift else value
                packed[piece] = jnp.where(lane // HALO == spot, value, packed[piece])
            out.append(packed)
        return out

    def place_edges(ref, places, west_values, east_values):
        for n, (c, row) in enumerate(places):
            piece, spot = divmod(n, per_piece)
            back = (LANES - HALO - spot * HALO) % LANES
            from_west = west_values[piece]
            from_west = pltpu.roll(from_west, back, 1) if back else from_west
            back = (LANES - spot * HALO) % LANES
            from_east = east_values[piece]
            from_east = pltpu.roll(from_east, back, 1) if back else from_east
            ref[c, tiles, pl.ds(row, 8), :] = beyond(from_west, from_east)

    def sideways(sends, gets, sems):
        return (
            remote(sends.at[0], gets.at[1], sems.at[0, 0], sems.at[0, 1], west),
            remote(sends.at[1], gets.at[0], sems.at[1, 0], sems.at[1, 1], east),
        )

    field_columns = sideways(ew_send, ew_recv, ew_sems)
    field_places = [(f, HALO + 8 * n) for f in range(FIELDS) for n in range(all_strips)]
    field_pieces = range(ew_recv.shape[1])
    every = tiles + 1
    relay = {t: (row_of(t) > g) == (odd == 1) for t in cross}

    def cross_message(t, q, relaying):
        @pl.when(relay[t] if relaying else jnp.logical_not(relay[t]))
        def _():
            received = [arrived(gets["y", i, t, q]) for i in others]
            send = sends["c", t, q]
            if relaying:
                received.append(arrived(gets["x", t, q]))
            coded(summed(0, t, q, received), send)
            if relaying:
                start(message(send, gets["z", t // 2, q], (s, row_of(t), x)))
            else:
                start(message(send, gets["x", t, q], mate))

    def statics():
        for copy in static_copies:
            copy.wait()

        @pl.loop(0, tile_rows // 8)
        def _(i):
            at = pl.ds(pl.multiple_of(i * 8, 8), 8)
            to = pl.ds(pl.multiple_of(i * 8 + top, 8), 8)
            for j in range(tiles):
                cols = pl.ds(j * LANES, LANES)
                for f in range(2):
                    fields[U + f, j, to, :] = vel_in[f, at, cols]
                    fields[WX + f, j, to, :] = wind_in[f, at, cols]
                thick = thick_in[at, cols]
                ice = ice_in[at, cols].astype(jnp.float32)
                strength = jnp.exp(-4.0 * (1.0 - conc_in[at, cols])) * thick
                fields[GRIP, j, to, :] = strength * ice * (1.0 / 3.0)
                fields[MASS, j, to, :] = thick * (ice * land_in[at, cols].astype(jnp.float32))

        pack_rows(0)
        pack_rows(1)

        @pl.when(has_north)
        def _():
            start(rows_up())

        @pl.when(has_south)
        def _():
            start(rows_down())

    def field_halo():
        place_rows(0, has_north, rows_down)
        place_rows(1, has_south, rows_up)

        @pl.when(has_north)
        def _():
            for copy in rows_up():
                copy.wait_send()

        @pl.when(has_south)
        def _():
            for copy in rows_down():
                copy.wait_send()

        for side, packed in enumerate(edges_of(fields, field_places)):
            for piece, value in enumerate(packed):
                ew_send[side, piece] = value
        start(field_columns)

    def margins(target, count):
        zero = jnp.zeros((8, LANES), jnp.float32)
        for f in range(count):
            for j in range(every):
                target[f, j, pl.ds(0, HALO), :] = zero
                target[f, j, pl.ds(end + HALO, HALO), :] = zero

    def sides(values):
        before = [pltpu.roll(value, 1, 1) for value in values]
        after = [pltpu.roll(value, LANES - 1, 1) for value in values]
        out = []
        for j in range(every):
            low = jnp.where(lane == 0, before[j - 1], before[j])
            high = jnp.where(lane == LANES - 1, after[(j + 1) % every], after[j])
            out.append(0.5 * (high - low))
        return out

    def strip_rows(i, shift):
        if shift == 0:
            return pl.ds(pl.multiple_of(i * 8 + HALO, 8), 8)
        return pl.ds(i * 8 + HALO + shift, 8)

    def rows_of(ref, f, at):
        return [ref[f, j, at, :] for j in range(every)]

    def stress_step(first, low, high):
        @pl.loop(low, high, unroll=True)
        def _(i):
            at, up, down = strip_rows(i, 0), strip_rows(i, -1), strip_rows(i, 1)
            east_u = sides(rows_of(fields, U, at))
            east_v = sides(rows_of(fields, V, at))
            for j in range(every):
                north_u = 0.5 * (fields[U, j, down, :] - fields[U, j, up, :])
                north_v = 0.5 * (fields[V, j, down, :] - fields[V, j, up, :])
                spread = east_u[j] + north_v
                tension = east_u[j] - north_v
                shear = north_u + east_v[j]
                turned = lax.rsqrt(
                    spread * spread + 0.25 * (tension * tension + shear * shear) + 0.01
                )
                grip = fields[GRIP, j, at, :]
                rate = grip * turned
                new0 = rate * spread - grip
                new1 = (0.25 * rate) * tension
                new2 = (0.125 * rate) * shear
                if not first:
                    new0 = stress[0, j, at, :] * (1.0 / 1.5) + new0
                    new1 = stress[1, j, at, :] * (1.0 / 1.5) + new1
                    new2 = stress[2, j, at, :] * (1.0 / 1.5) + new2
                stress[0, j, at, :] = new0
                stress[1, j, at, :] = new1
                stress[2, j, at, :] = new2

    def velocity_step(low, high, width):
        @pl.loop(low, high, unroll=True)
        def _(i):
            at, up, down = strip_rows(i, 0), strip_rows(i, -1), strip_rows(i, 1)
            first = rows_of(stress, 0, at)
            second = rows_of(stress, 1, at)
            east_normal = sides([0.5 * (a + b) for a, b in zip(first, second)])
            east_third = sides(rows_of(stress, 2, at))
            for j in range(width):
                north_third = 0.5 * (stress[2, j, down, :] - stress[2, j, up, :])
                north_normal = 0.25 * (
                    (stress[0, j, down, :] - stress[1, j, down, :])
                    - (stress[0, j, up, :] - stress[1, j, up, :])
                )
                u, v = fields[U, j, at, :], fields[V, j, at, :]
                cx, cy = surf[0, j, at, :], surf[1, j, at, :]
                mass = fields[MASS, j, at, :]
                rel_u, rel_v = cx - u, cy - v
                drag = 0.8 * jnp.sqrt(rel_u * rel_u + rel_v * rel_v)
                a = mass + drag
                b = 0.5 * mass
                rx = mass * u + (east_normal[j] + north_third) + drag * cx + fields[WX, j, at, :]
                ry = mass * v + (east_third[j] + north_normal) + drag * cy + fields[WY, j, at, :]
                live = mass > 0.0
                inverse = 1.0 / jnp.where(live, a * a + b * b, 1.0)
                fields[U, j, at, :] = jnp.where(live, (a * rx + b * ry) * inverse, 0.0)
                fields[V, j, at, :] = jnp.where(live, (a * ry - b * rx) * inverse, 0.0)

    def first_stress():
        for copy in field_columns:
            copy.wait()
        place_edges(
            fields,
            field_places,
            [ew_recv[0, piece] for piece in field_pieces],
            [ew_recv[1, piece] for piece in field_pieces],
        )
        margins(fields, 2)
        margins(stress, 3)
        margins(surf, 3)
        stress_step(True, 0, all_strips)

    norm = 1.0 / math.sqrt(levels)
    chunk_strips = size // 8
    pieces = side_send.shape[2]
    first_rows, last_rows = pl.ds(top, HALO), pl.ds(end - HALO, HALO)

    def halo(side):
        sent, got = ns_surf_send.at[side], ns_surf.at[1 - side]
        devices = (south, south_west, south_east) if side else (north, north_west, north_east)
        return [
            remote(sent, got, surf_sems.at[side, 0, 0], surf_sems.at[side, 0, 1], devices[0]),
            remote(
                sent.at[:, 0],
                corner_recv.at[1 - side, 1],
                surf_sems.at[side, 1, 0],
                surf_sems.at[side, 1, 1],
                devices[1],
            ),
            remote(
                sent.at[:, tiles - 1],
                corner_recv.at[1 - side, 0],
                surf_sems.at[side, 2, 0],
                surf_sems.at[side, 2, 1],
                devices[2],
            ),
        ]

    def inside(q):
        return [(c, top + q * size + 8 * n) for c in range(3) for n in range(chunk_strips)]

    def side_copies(q):
        return (
            remote(side_send.at[q, 0], side_recv.at[q, 1], side_sends_sem, side_sems.at[q, 1], west),
            remote(side_send.at[q, 1], side_recv.at[q, 0], side_sends_sem, side_sems.at[q, 0], east),
        )

    def surface(q):
        need(0, 0, q)
        received = [arrived(gets["y", i, 0, q]) for i in others]
        received.append(arrived(gets["p", q]))
        received += [arrived(gets["z", m, q]) for m in range(1, pairs)]
        parts = summed(0, 0, q, received)
        for c in range(3):
            value_of = parts(c)
            for n in range(strips):
                for j in range(tiles):
                    to = pl.ds(top + q * size + n * 16, 16)
                    surf[c, j, to, :] = value_of(pl.ds(n * 16, 16), j) * norm
        for side, packed in enumerate(edges_of(surf, inside(q))):
            for piece in range(pieces):
                side_send[q, side, piece] = packed[piece]
        start(side_copies(q))
        for side, edge, rows in ((0, 0, first_rows), (1, CHUNKS - 1, last_rows)):
            if q == edge:
                for c in range(3):
                    for j in range(tiles):
                        ns_surf_send[side, c, j] = surf[c, j, rows, :]
        if q == 0:

            @pl.when(has_north)
            def _():
                start(halo(0))

        if q == CHUNKS - 1:

            @pl.when(has_south)
            def _():
                start(halo(1))

    def place_halo(side, has):
        to = pl.ds(end, HALO) if side else pl.ds(HALO, HALO)

        def there():
            for copy in halo(1 - side):
                copy.wait_recv()
            for c in range(3):
                for j in range(tiles):
                    surf[c, j, to, :] = ns_surf[side, c, j]
                surf[c, tiles, to, :] = beyond(corner_recv[side, 0, c], corner_recv[side, 1, c])

        def missing():
            for c in range(3):
                for j in range(every):
                    surf[c, j, to, :] = jnp.zeros((HALO, LANES), jnp.float32)

        either(has, there, missing)

    def surface_halo():
        place_halo(0, has_north)
        place_halo(1, has_south)

        @pl.when(has_north)
        def _():
            for copy in halo(0):
                copy.wait_send()

        @pl.when(has_south)
        def _():
            for copy in halo(1):
                copy.wait_send()

    def surface_sides(q):
        for copy in side_copies(q):
            copy.wait_recv()
        place_edges(
            surf,
            inside(q),
            [side_recv[q, 0, piece] for piece in range(pieces)],
            [side_recv[q, 1, piece] for piece in range(pieces)],
        )

    def slope_step(low, high):
        @pl.loop(low, high, unroll=True)
        def _(i):
            at, up, down = strip_rows(i, 0), strip_rows(i, -1), strip_rows(i, 1)
            slope_x = sides(rows_of(surf, 2, at))
            for j in range(every):
                slope_y = 0.5 * (surf[2, j, down, :] - surf[2, j, up, :])
                gain = -0.5 * fields[MASS, j, at, :]
                fields[WX, j, at, :] = fields[WX, j, at, :] + gain * slope_x[j]
                fields[WY, j, at, :] = fields[WY, j, at, :] + gain * slope_y

    halves = 2 * SUB - 1

    def half_step(h, low, high):
        if h == halves - 1:
            low, high = max(low, 1), min(high, all_strips - 1)
        low, high = max(low, 0), min(high, all_strips)
        if low >= high:
            return
        if h == 0:
            slope_step(low, high)
        if h % 2:
            stress_step(False, low, high)
        else:
            velocity_step(low, high, tiles if h == halves - 1 else every)

    late_low = 1 + order[-1] * chunk_strips - 1
    late_high = 1 + (order[-1] + 1) * chunk_strips + 1

    def early_steps(first, last):
        for h in range(first, last):
            half_step(h, 0, late_low - h)
            half_step(h, late_high + h, all_strips)

    def late_steps():
        for h in range(halves):
            half_step(h, late_low - h, late_high + h)

    for n, q in enumerate(order):
        for t in cross:
            need(0, t, q)
            cross_message(t, q, False)
        if n and order[n - 1] not in traded:
            send_p(order[n - 1])
        for t in cross:
            cross_message(t, q, True)
        if n == 0:
            statics()
            for late in traded:
                for i in others:
                    send_y(i, 0, late, [arrived(gets["a", i, late])])
                    start_y(i, 0, late)
        if n == CHUNKS // 2:
            field_halo()
        if n >= 2:
            surface(order[n - 2])
    if order[-1] not in traded:
        send_p(order[-1])
    first_stress()
    surface(order[-2])
    for q in order[:-2]:
        surface_sides(q)
    surface_sides(order[-2])
    for send_sem, source in ((send_sems.at[0], send_codes), (send_sems.at[1], send_scales)):
        remote(source, source, send_sem, recv_sems.at[0, 0], mate).wait_send()
    surface(order[-1])
    surface_halo()
    early_steps(0, halves)
    surface_sides(order[-1])
    late_steps()
    remote(side_send, side_recv, side_sends_sem, side_sems.at[0, 0], west).wait_send()


def write_out(fields, stress, vel_out, stress_out, sems):
    tiles = fields.shape[1] - 1
    rows = pl.ds(2 * HALO, vel_out.shape[1])
    copies = []
    for j in range(tiles):
        cols = pl.ds(j * LANES, LANES)
        for n, (source, target) in enumerate(
            ((fields.at[pl.ds(U, 2)], vel_out), (stress, stress_out))
        ):
            copy = pltpu.make_async_copy(
                source.at[:, j, rows, :], target.at[:, :, cols], sems.at[n, j]
            )
            copy.start()
            copies.append(copy)
    for copy in copies:
        copy.wait()


def body(
    ocean, level_weight, velocity_start, wind_stress, thickness, concentration, ice_mask, land_mask
):
    secs, rows_g, cols_g = lax.axis_size("sec"), lax.axis_size("gy"), lax.axis_size("gx")
    held = ocean.shape[0]
    rows, cols = thickness.shape
    tiles = cols // LANES
    tall = rows + 4 * HALO
    wide_rows = rows + 2 * HALO
    size = rows // CHUNKS
    pieces = pl.cdiv(3 * (size // 8), LANES // HALO)
    field_pieces = pl.cdiv(FIELDS * (wide_rows // 8), LANES // HALO)
    f32, i16 = jnp.float32, jnp.int16
    dma = pltpu.SemaphoreType.DMA
    anywhere = pl.BlockSpec(memory_space=pl.ANY)
    on_chip = pl.BlockSpec(memory_space=pltpu.VMEM)
    sends, gets = numbered(secs, rows_g)
    fields, stress = pl.pallas_call(
        functools.partial(kernel, (secs, rows_g, cols_g, level_weight.shape[0])),
        out_shape=(
            pltpu.VMEM((FIELDS, tiles + 1, tall, LANES), f32),
            pltpu.VMEM((3, tiles + 1, tall, LANES), f32),
        ),
        in_specs=[anywhere] * 8,
        out_specs=(on_chip, on_chip),
        scratch_shapes=[
            pltpu.VMEM((secs * rows_g, held, 3, rows, cols), ocean.dtype),
            pltpu.VMEM((len(sends), 3, size, cols), i16),
            pltpu.VMEM((len(sends), 3, LANES), f32),
            pltpu.VMEM((len(gets), 3, size, cols), i16),
            pltpu.VMEM((len(gets), 3, LANES), f32),
            pltpu.VMEM((2, rows, cols), f32),
            pltpu.VMEM((2, rows, cols), f32),
            pltpu.VMEM((rows, cols), f32),
            pltpu.VMEM((rows, cols), f32),
            pltpu.VMEM((rows, cols), jnp.int32),
            pltpu.VMEM((rows, cols), jnp.int32),
            pltpu.VMEM((3, tiles + 1, tall, LANES), f32),
            pltpu.VMEM((2, FIELDS * HALO, cols), i16),
            pltpu.VMEM((2, FIELDS, LANES), f32),
            pltpu.VMEM((2, FIELDS * HALO, cols), i16),
            pltpu.VMEM((2, FIELDS, LANES), f32),
            pltpu.VMEM((2, field_pieces, 8, LANES), f32),
            pltpu.VMEM((2, field_pieces, 8, LANES), f32),
            pltpu.VMEM((2, 3, tiles, HALO, LANES), f32),
            pltpu.VMEM((2, 3, tiles, HALO, LANES), f32),
            pltpu.VMEM((CHUNKS, 2, pieces, 8, LANES), f32),
            pltpu.VMEM((CHUNKS, 2, pieces, 8, LANES), f32),
            pltpu.VMEM((2, 2, 3, HALO, LANES), f32),
            pltpu.SMEM(level_weight.shape, f32),
            dma(()),
            dma((secs - 1, rows_g - 2)),
            dma((secs * rows_g,)),
            dma((6,)),
            dma((2,)),
            dma((len(gets), 2)),
            dma((2, 2, 2)),
            dma((2, 2)),
            dma((2, 3, 2)),
            dma(()),
            dma((CHUNKS, 2)),
            pltpu.SemaphoreType.REGULAR((rows_g,)),
        ],
        compiler_params=pltpu.CompilerParams(
            collective_id=0, has_side_effects=True, vmem_limit_bytes=52 * 1024 * 1024
        ),
    )(
        level_weight,
        ocean,
        velocity_start,
        wind_stress,
        thickness,
        concentration,
        ice_mask,
        land_mask,
    )
    return pl.pallas_call(
        write_out,
        out_shape=(
            jax.ShapeDtypeStruct((2, rows, cols), f32),
            jax.ShapeDtypeStruct((3, rows, cols), f32),
        ),
        in_specs=[on_chip, on_chip],
        out_specs=(anywhere, anywhere),
        scratch_shapes=[dma((2, tiles))],
        compiler_params=pltpu.CompilerParams(vmem_limit_bytes=VMEM_OUT),
    )(fields, stress)


def solution(mesh):
    placed = (
        P(("sec", "gy"), None, None, "gx"),
        P(),
        P(None, ("sec", "gy"), "gx"),
        P(None, ("sec", "gy"), "gx"),
        P(("sec", "gy"), "gx"),
        P(("sec", "gy"), "gx"),
        P(("sec", "gy"), "gx"),
        P(("sec", "gy"), "gx"),
    )
    return jax.shard_map(
        body,
        mesh=mesh,
        in_specs=placed,
        out_specs=(P(None, ("sec", "gy"), "gx"), P(None, ("sec", "gy"), "gx")),
        check_vma=False,
    )
```

```python
import functools
import math

import jax
import jax.numpy as jnp
from jax import lax
from jax.experimental import pallas as pl
from jax.experimental.pallas import tpu as pltpu
from jax.sharding import PartitionSpec as P

SUB = 4
HALO = 8
CHUNKS = 4
PLAIN = 4
LEAD = 2
VMEM_OUT = 8 * 1024 * 1024
LANES = 128
MESH = pl.DeviceIdType.MESH

U, V, WX, WY, MASS, GRIP = range(6)
FIELDS = 6


def chunk_order():
    return [0, CHUNKS - 1] + list(range(1, CHUNKS - 1))


def numbered(secs, rows_g):
    order = chunk_order()
    others, cross = range(1, secs), range(2, rows_g)
    sends, gets = {}, {}
    for q in order:
        for i in others:
            for t in [0] + ([1] if q in order[:PLAIN] else []) + list(cross):
                sends["y", i, t, q] = len(sends)
                gets["y", i, t, q] = len(gets)
            if q in order[PLAIN:]:
                sends["a", i, q] = len(sends)
                gets["a", i, q] = len(gets)
        sends["p", q] = len(sends)
        gets["p", q] = len(gets)
        for t in cross:
            sends["c", t, q] = len(sends)
            gets["x", t, q] = len(gets)
        for m in range(1, rows_g // 2):
            gets["z", m, q] = len(gets)
    return sends, gets


def kernel(
    dims,
    weight_hbm,
    ocean_hbm,
    vel_hbm,
    wind_hbm,
    thick_hbm,
    conc_hbm,
    ice_hbm,
    land_hbm,
    fields,
    stress,
    ocean,
    send_codes,
    send_scales,
    recv_codes,
    recv_scales,
    vel_in,
    wind_in,
    thick_in,
    conc_in,
    ice_in,
    land_in,
    surf,
    ns_codes,
    ns_scales,
    ns_got,
    ns_scales_got,
    ew_send,
    ew_recv,
    ns_surf_send,
    ns_surf,
    side_send,
    side_recv,
    corner_recv,
    weight_ref,
    weight_sem,
    first_sems,
    ocean_sems,
    static_sems,
    send_sems,
    recv_sems,
    ns_sems,
    ew_sems,
    surf_sems,
    side_sends_sem,
    side_sems,
    gate,
):
    secs, rows_g, cols_g, levels = dims
    held = ocean_hbm.shape[0]
    tile_rows, tile_cols = thick_hbm.shape
    tiles = tile_cols // LANES
    top = 2 * HALO
    end = top + tile_rows
    size = tile_rows // CHUNKS
    pairs = rows_g // 2
    s, g, x = lax.axis_index("sec"), lax.axis_index("gy"), lax.axis_index("gx")
    ranks = secs * rows_g
    rank = s * rows_g + g
    pair = g // 2
    odd = lax.rem(g, 2)

    def at_rank(number):
        number = lax.rem(number + ranks, ranks)
        return (number // rows_g, lax.rem(number, rows_g), x)

    def row_of(t):
        if t == 0:
            return g
        if t == 1:
            return g + 1 - 2 * odd
        return 2 * lax.rem(pair + t // 2, pairs) + t % 2

    north, south = at_rank(rank - 1), at_rank(rank + 1)
    west = (s, g, lax.rem(x + cols_g - 1, cols_g))
    east = (s, g, lax.rem(x + 1, cols_g))
    north_west, north_east = north[:2] + west[2:], north[:2] + east[2:]
    south_west, south_east = south[:2] + west[2:], south[:2] + east[2:]
    over_secs = [(lax.rem(s + i, secs), g, x) for i in range(1, secs)]
    mate = (s, row_of(1), x)
    others = range(1, secs)
    cross = range(2, rows_g)
    order = chunk_order()
    traded = order[PLAIN:]
    sends, gets = numbered(secs, rows_g)

    weight_copy = pltpu.make_async_copy(weight_hbm, weight_ref, weight_sem)
    weight_copy.start()
    reads = {}

    def read(key, i, t, first, count, sem):
        block = lax.rem(s + i, secs) * rows_g + row_of(t)
        at = pl.ds(pl.multiple_of(block * tile_rows + first, 16), count)
        copy = pltpu.make_async_copy(
            ocean_hbm.at[:, :, at, :],
            ocean.at[i * rows_g + t, :, :, pl.ds(first, count), :],
            sem,
        )
        copy.start()
        reads[key] = copy

    def read_whole(i, t):
        read((i, t), i, t, 0, tile_rows, ocean_sems.at[i * rows_g + t])

    for i in others:
        for t in cross:
            read((i, t, 0), i, t, 0, size, first_sems.at[i - 1, t - 2])

    def greet(semaphore, devices):
        for device in devices + over_secs:
            pl.semaphore_signal(semaphore, inc=1, device_id=device, device_id_type=MESH)

        @pl.when(g > 0)
        def _():
            above = (s, g - 1, x)
            pl.semaphore_signal(semaphore, inc=1, device_id=above, device_id_type=MESH)

        @pl.when(g < rows_g - 1)
        def _():
            below = (s, g + 1, x)
            pl.semaphore_signal(semaphore, inc=1, device_id=below, device_id_type=MESH)

    in_line = jnp.where(g > 0, 1, 0) + jnp.where(g < rows_g - 1, 1, 0)
    barrier = pltpu.get_barrier_semaphore()
    greet(barrier, [west, east])
    weight_copy.wait()
    own_weights = [weight_ref[rank * held + k] for k in range(held)]
    strips = size // 16

    def need(i, t, q):
        key = (i, t, 0) if q == 0 and (i, t, 0) in firsts else (i, t)
        if key in reads:
            reads.pop(key).wait()

    firsts = set(reads)
    static_copies = []

    def read_rest():
        for i in others:
            for t in cross:
                read((i, t), i, t, size, tile_rows - size, ocean_sems.at[i * rows_g + t])
        for i in others:
            read_whole(i, 1)
        read_whole(0, 1)
        for i in others:
            read_whole(i, 0)
        for t in cross:
            read_whole(0, t)
        for n, (source, target) in enumerate(
            (
                (vel_hbm, vel_in),
                (wind_hbm, wind_in),
                (thick_hbm, thick_in),
                (conc_hbm, conc_in),
                (ice_hbm, ice_in),
                (land_hbm, land_in),
            )
        ):
            copy = pltpu.make_async_copy(source, target, static_sems.at[n])
            copy.start()
            static_copies.append(copy)
        read_whole(0, 0)

    def remote(source, target, send_sem, recv_sem, device):
        return pltpu.make_async_remote_copy(
            src_ref=source,
            dst_ref=target,
            send_sem=send_sem,
            recv_sem=recv_sem,
            device_id=device,
            device_id_type=MESH,
        )

    def message(send, get, device):
        return (
            remote(
                send_codes.at[send], recv_codes.at[get], send_sems.at[0], recv_sems.at[get, 0], device
            ),
            remote(
                send_scales.at[send], recv_scales.at[get], send_sems.at[1], recv_sems.at[get, 1], device
            ),
        )

    def start(copies):
        for copy in copies:
            copy.start()

    def arrived(get):
        for copy in message(0, get, mate):
            copy.wait_recv()
        return recv_codes.at[get], recv_scales.at[get]

    def level_sum(i, t, q, c, at, j):
        rows = pl.ds(q * size + at.start, 16)
        cols = pl.ds(j * LANES, LANES)
        slot = i * rows_g + t
        value = own_weights[0] * ocean[slot, 0, c, rows, cols].astype(jnp.float32)
        for k in range(1, held):
            value = value + own_weights[k] * ocean[slot, k, c, rows, cols].astype(jnp.float32)
        return value

    def decoded(codes, scale, c, at, j):
        code = codes[c, at, pl.ds(j * LANES, LANES)].astype(jnp.int32)
        return code.astype(jnp.float32) * scale

    def summed(i, t, q, received):
        def parts(c):
            scales = [scale[pl.ds(c, 1), :] for _, scale in received]

            def value_of(at, j):
                value = level_sum(i, t, q, c, at, j)
                for (codes, _), scale in zip(received, scales):
                    value = value + decoded(codes, scale, c, at, j)
                return value

            return value_of

        return parts

    def coded(parts, send):
        for c in range(3):
            value_of = parts(c)
            values = {}
            most = None
            for n in range(strips):
                at = pl.ds(n * 16, 16)
                for j in range(tiles):
                    value = value_of(at, j)
                    values[n, j] = value
                    size_of = jnp.abs(value)
                    most = size_of if most is None else jnp.maximum(most, size_of)
            most = jnp.maximum(jnp.max(most, axis=0, keepdims=True), 1e-30)
            send_scales[send, pl.ds(c, 1), :] = most * (1.0 / 32767.0)
            inverse = 32767.0 / most
            for (n, j), value in values.items():
                code = jnp.round(value * inverse)
                send_codes[send, c, pl.ds(n * 16, 16), pl.ds(j * LANES, LANES)] = code.astype(
                    jnp.int32
                ).astype(jnp.int16)

    def send_y(i, t, q, received):
        need(i, t, q)
        coded(summed(i, t, q, received), sends["y", i, t, q])

    def start_y(i, t, q):
        start(message(sends["y", i, t, q], gets["y", i, t, q], over_secs[i - 1]))

    def send_p(q):
        need(0, 1, q)
        received = []
        if q not in traded:
            received = [arrived(gets["y", i, 1, q]) for i in others]
        coded(summed(0, 1, q, received), sends["p", q])
        start(message(sends["p", q], gets["p", q], mate))

    def send_a(q):
        for i in others:
            need(i, 1, q)
            coded(summed(i, 1, q, []), sends["a", i, q])
            start(message(sends["a", i, q], gets["a", i, q], mate))

    floods = rows_g
    flooded = 0

    def flood_to(number):
        nonlocal flooded
        while flooded < number:
            pl.semaphore_wait(gate.at[flooded], secs + 1 + in_line)
            flooded += 1
            if flooded < floods:
                greet(gate.at[flooded], [west, east])

    plan = [[(t, q) for t in cross] for q in order[:LEAD]]
    for n, q in enumerate(order):
        if n + LEAD < len(order):
            plan.append([(1, q)] * (q not in traded))
            plan.append([(t, order[n + LEAD]) for t in cross])
            plan.append([(0, q)] * (q not in traded))
        else:
            plan.append([(t, q) for t in (1, 0)] * (q not in traded))
    begun = False
    for n, group in enumerate(plan):
        if n:
            flood_to(min(n, floods))
        if n == 2:
            for q in traded:
                send_a(q)
            for q in traded:
                send_p(q)
        for t, q in group:
            for i in others:
                send_y(i, t, q, [])
                if not begun:
                    read_rest()
                    pl.semaphore_wait(barrier, secs + 1 + in_line)
                start_y(i, t, q)
                if not begun:
                    greet(gate.at[0], [west, east])
                    begun = True
    flood_to(floods)

    has_north, has_south = rank > 0, rank < ranks - 1

    def rows_up():
        return (
            remote(ns_codes.at[0], ns_got.at[1], ns_sems.at[0, 0, 0], ns_sems.at[0, 0, 1], north),
            remote(ns_scales.at[0], ns_scales_got.at[1], ns_sems.at[0, 1, 0], ns_sems.at[0, 1, 1], north),
        )

    def rows_down():
        return (
            remote(ns_codes.at[1], ns_got.at[0], ns_sems.at[1, 0, 0], ns_sems.at[1, 0, 1], south),
            remote(ns_scales.at[1], ns_scales_got.at[0], ns_sems.at[1, 1, 0], ns_sems.at[1, 1, 1], south),
        )

    def pack_rows(side):
        rows = pl.ds(end - HALO, HALO) if side else pl.ds(top, HALO)
        for f in range(0, FIELDS, 2):
            inverses = []
            for k in (f, f + 1):
                most = jnp.abs(fields[k, 0, rows, :])
                for j in range(1, tiles):
                    most = jnp.maximum(most, jnp.abs(fields[k, j, rows, :]))
                most = jnp.maximum(jnp.max(most, axis=0, keepdims=True), 1e-30)
                ns_scales[side, pl.ds(k, 1), :] = most * (1.0 / 32767.0)
                inverses.append(jnp.broadcast_to(32767.0 / most, (HALO, LANES)))
            inverse = jnp.concatenate(inverses, axis=0)
            for j in range(tiles):
                value = jnp.concatenate([fields[f, j, rows, :], fields[f + 1, j, rows, :]], axis=0)
                code = jnp.round(value * inverse).astype(jnp.int32).astype(jnp.int16)
                ns_codes[side, pl.ds(f * HALO, 2 * HALO), pl.ds(j * LANES, LANES)] = code

    def either(condition, yes, no):
        pl.when(condition)(yes)
        pl.when(jnp.logical_not(condition))(no)

    def place_rows(side, has, copies):
        to = pl.ds(end, HALO) if side else pl.ds(HALO, HALO)

        def there():
            for copy in copies():
                copy.wait_recv()
            for f in range(0, FIELDS, 2):
                scales = [ns_scales_got[side, pl.ds(k, 1), :] for k in (f, f + 1)]
                for j in range(tiles):
                    code = ns_got[side, pl.ds(f * HALO, 2 * HALO), pl.ds(j * LANES, LANES)]
                    value = code.astype(jnp.int32).astype(jnp.float32)
                    fields[f, j, to, :] = value[0:HALO] * scales[0]
                    fields[f + 1, j, to, :] = value[HALO : 2 * HALO] * scales[1]

        def missing():
            for f in range(FIELDS):
                for j in range(tiles):
                    fields[f, j, to, :] = jnp.zeros((HALO, LANES), jnp.float32)

        either(has, there, missing)

    lane = lax.broadcasted_iota(jnp.int32, (8, LANES), 1)
    all_strips = (tile_rows + 2 * HALO) // 8

    def beyond(west_value, east_value):
        return jnp.where(
            lane < HALO, east_value, jnp.where(lane >= LANES - HALO, west_value, 0.0)
        )

    per_piece = LANES // HALO

    def edges_of(ref, places):
        out = []
        for j, offset in ((0, 0), (tiles - 1, HALO)):
            packed = [jnp.zeros((8, LANES), jnp.float32)] * pl.cdiv(len(places), per_piece)
            for n, (c, row) in enumerate(places):
                piece, spot = divmod(n, per_piece)
                value = ref[c, j, pl.ds(row, 8), :]
                shift = (spot * HALO + offset) % LANES
                value = pltpu.roll(value, shift, 1) if shift else value
                packed[piece] = jnp.where(lane // HALO == spot, value, packed[piece])
            out.append(packed)
        return out

    def place_edges(ref, places, west_values, east_values):
        for n, (c, row) in enumerate(places):
            piece, spot = divmod(n, per_piece)
            back = (LANES - HALO - spot * HALO) % LANES
            from_west = west_values[piece]
            from_west = pltpu.roll(from_west, back, 1) if back else from_west
            back = (LANES - spot * HALO) % LANES
            from_east = east_values[piece]
            from_east = pltpu.roll(from_east, back, 1) if back else from_east
            ref[c, tiles, pl.ds(row, 8), :] = beyond(from_west, from_east)

    def sideways(sends, gets, sems):
        return (
            remote(sends.at[0], gets.at[1], sems.at[0, 0], sems.at[0, 1], west),
            remote(sends.at[1], gets.at[0], sems.at[1, 0], sems.at[1, 1], east),
        )

    field_columns = sideways(ew_send, ew_recv, ew_sems)
    field_places = [(f, HALO + 8 * n) for f in range(FIELDS) for n in range(all_strips)]
    field_pieces = range(ew_recv.shape[1])
    every = tiles + 1
    relay = {t: (row_of(t) > g) == (odd == 1) for t in cross}

    def cross_message(t, q, relaying):
        @pl.when(relay[t] if relaying else jnp.logical_not(relay[t]))
        def _():
            received = [arrived(gets["y", i, t, q]) for i in others]
            send = sends["c", t, q]
            if relaying:
                received.append(arrived(gets["x", t, q]))
            coded(summed(0, t, q, received), send)
            if relaying:
                start(message(send, gets["z", t // 2, q], (s, row_of(t), x)))
            else:
                start(message(send, gets["x", t, q], mate))

    def statics():
        for copy in static_copies:
            copy.wait()

        @pl.loop(0, tile_rows // 8)
        def _(i):
            at = pl.ds(pl.multiple_of(i * 8, 8), 8)
            to = pl.ds(pl.multiple_of(i * 8 + top, 8), 8)
            for j in range(tiles):
                cols = pl.ds(j * LANES, LANES)
                for f in range(2):
                    fields[U + f, j, to, :] = vel_in[f, at, cols]
                    fields[WX + f, j, to, :] = wind_in[f, at, cols]
                thick = thick_in[at, cols]
                ice = ice_in[at, cols].astype(jnp.float32)
                strength = jnp.exp(-4.0 * (1.0 - conc_in[at, cols])) * thick
                fields[GRIP, j, to, :] = strength * ice * (1.0 / 3.0)
                fields[MASS, j, to, :] = thick * (ice * land_in[at, cols].astype(jnp.float32))

        pack_rows(0)
        pack_rows(1)

        @pl.when(has_north)
        def _():
            start(rows_up())

        @pl.when(has_south)
        def _():
            start(rows_down())

    def field_halo():
        place_rows(0, has_north, rows_down)
        place_rows(1, has_south, rows_up)

        @pl.when(has_north)
        def _():
            for copy in rows_up():
                copy.wait_send()

        @pl.when(has_south)
        def _():
            for copy in rows_down():
                copy.wait_send()

        for side, packed in enumerate(edges_of(fields, field_places)):
            for piece, value in enumerate(packed):
                ew_send[side, piece] = value
        start(field_columns)

    def margins(target, count):
        zero = jnp.zeros((8, LANES), jnp.float32)
        for f in range(count):
            for j in range(every):
                target[f, j, pl.ds(0, HALO), :] = zero
                target[f, j, pl.ds(end + HALO, HALO), :] = zero

    def sides(values):
        before = [pltpu.roll(value, 1, 1) for value in values]
        after = [pltpu.roll(value, LANES - 1, 1) for value in values]
        out = []
        for j in range(every):
            low = jnp.where(lane == 0, before[j - 1], before[j])
            high = jnp.where(lane == LANES - 1, after[(j + 1) % every], after[j])
            out.append(0.5 * (high - low))
        return out

    def strip_rows(i, shift):
        if shift == 0:
            return pl.ds(pl.multiple_of(i * 8 + HALO, 8), 8)
        return pl.ds(i * 8 + HALO + shift, 8)

    def rows_of(ref, f, at):
        return [ref[f, j, at, :] for j in range(every)]

    def stress_step(first, low, high):
        @pl.loop(low, high, unroll=True)
        def _(i):
            at, up, down = strip_rows(i, 0), strip_rows(i, -1), strip_rows(i, 1)
            east_u = sides(rows_of(fields, U, at))
            east_v = sides(rows_of(fields, V, at))
            for j in range(every):
                north_u = 0.5 * (fields[U, j, down, :] - fields[U, j, up, :])
                north_v = 0.5 * (fields[V, j, down, :] - fields[V, j, up, :])
                spread = east_u[j] + north_v
                tension = east_u[j] - north_v
                shear = north_u + east_v[j]
                turned = lax.rsqrt(
                    spread * spread + 0.25 * (tension * tension + shear * shear) + 0.01
                )
                grip = fields[GRIP, j, at, :]
                rate = grip * turned
                new0 = rate * spread - grip
                new1 = (0.25 * rate) * tension
                new2 = (0.125 * rate) * shear
                if not first:
                    new0 = stress[0, j, at, :] * (1.0 / 1.5) + new0
                    new1 = stress[1, j, at, :] * (1.0 / 1.5) + new1
                    new2 = stress[2, j, at, :] * (1.0 / 1.5) + new2
                stress[0, j, at, :] = new0
                stress[1, j, at, :] = new1
                stress[2, j, at, :] = new2

    def velocity_step(low, high, width):
        @pl.loop(low, high, unroll=True)
        def _(i):
            at, up, down = strip_rows(i, 0), strip_rows(i, -1), strip_rows(i, 1)
            first = rows_of(stress, 0, at)
            second = rows_of(stress, 1, at)
            east_normal = sides([0.5 * (a + b) for a, b in zip(first, second)])
            east_third = sides(rows_of(stress, 2, at))
            for j in range(width):
                north_third = 0.5 * (stress[2, j, down, :] - stress[2, j, up, :])
                north_normal = 0.25 * (
                    (stress[0, j, down, :] - stress[1, j, down, :])
                    - (stress[0, j, up, :] - stress[1, j, up, :])
                )
                u, v = fields[U, j, at, :], fields[V, j, at, :]
                cx, cy = surf[0, j, at, :], surf[1, j, at, :]
                mass = fields[MASS, j, at, :]
                rel_u, rel_v = cx - u, cy - v
                drag = 0.8 * jnp.sqrt(rel_u * rel_u + rel_v * rel_v)
                a = mass + drag
                b = 0.5 * mass
                rx = mass * u + (east_normal[j] + north_third) + drag * cx + fields[WX, j, at, :]
                ry = mass * v + (east_third[j] + north_normal) + drag * cy + fields[WY, j, at, :]
                live = mass > 0.0
                inverse = 1.0 / jnp.where(live, a * a + b * b, 1.0)
                fields[U, j, at, :] = jnp.where(live, (a * rx + b * ry) * inverse, 0.0)
                fields[V, j, at, :] = jnp.where(live, (a * ry - b * rx) * inverse, 0.0)

    def first_stress():
        for copy in field_columns:
            copy.wait()
        place_edges(
            fields,
            field_places,
            [ew_recv[0, piece] for piece in field_pieces],
            [ew_recv[1, piece] for piece in field_pieces],
        )
        margins(fields, 2)
        margins(stress, 3)
        margins(surf, 3)
        stress_step(True, 0, all_strips)

    norm = 1.0 / math.sqrt(levels)
    chunk_strips = size // 8
    pieces = side_send.shape[2]
    first_rows, last_rows = pl.ds(top, HALO), pl.ds(end - HALO, HALO)

    def halo(side):
        sent, got = ns_surf_send.at[side], ns_surf.at[1 - side]
        devices = (south, south_west, south_east) if side else (north, north_west, north_east)
        return [
            remote(sent, got, surf_sems.at[side, 0, 0], surf_sems.at[side, 0, 1], devices[0]),
            remote(
                sent.at[:, 0],
                corner_recv.at[1 - side, 1],
                surf_sems.at[side, 1, 0],
                surf_sems.at[side, 1, 1],
                devices[1],
            ),
            remote(
                sent.at[:, tiles - 1],
                corner_recv.at[1 - side, 0],
                surf_sems.at[side, 2, 0],
                surf_sems.at[side, 2, 1],
                devices[2],
            ),
        ]

    def inside(q):
        return [(c, top + q * size + 8 * n) for c in range(3) for n in range(chunk_strips)]

    def side_copies(q):
        return (
            remote(side_send.at[q, 0], side_recv.at[q, 1], side_sends_sem, side_sems.at[q, 1], west),
            remote(side_send.at[q, 1], side_recv.at[q, 0], side_sends_sem, side_sems.at[q, 0], east),
        )

    def surface(q):
        need(0, 0, q)
        received = [arrived(gets["y", i, 0, q]) for i in others]
        received.append(arrived(gets["p", q]))
        received += [arrived(gets["z", m, q]) for m in range(1, pairs)]
        parts = summed(0, 0, q, received)
        for c in range(3):
            value_of = parts(c)
            for n in range(strips):
                for j in range(tiles):
                    to = pl.ds(top + q * size + n * 16, 16)
                    surf[c, j, to, :] = value_of(pl.ds(n * 16, 16), j) * norm
        for side, packed in enumerate(edges_of(surf, inside(q))):
            for piece in range(pieces):
                side_send[q, side, piece] = packed[piece]
        start(side_copies(q))
        for side, edge, rows in ((0, 0, first_rows), (1, CHUNKS - 1, last_rows)):
            if q == edge:
                for c in range(3):
                    for j in range(tiles):
                        ns_surf_send[side, c, j] = surf[c, j, rows, :]
        if q == 0:

            @pl.when(has_north)
            def _():
                start(halo(0))

        if q == CHUNKS - 1:

            @pl.when(has_south)
            def _():
                start(halo(1))

    def place_halo(side, has):
        to = pl.ds(end, HALO) if side else pl.ds(HALO, HALO)

        def there():
            for copy in halo(1 - side):
                copy.wait_recv()
            for c in range(3):
                for j in range(tiles):
                    surf[c, j, to, :] = ns_surf[side, c, j]
                surf[c, tiles, to, :] = beyond(corner_recv[side, 0, c], corner_recv[side, 1, c])

        def missing():
            for c in range(3):
                for j in range(every):
                    surf[c, j, to, :] = jnp.zeros((HALO, LANES), jnp.float32)

        either(has, there, missing)

    def surface_halo():
        place_halo(0, has_north)
        place_halo(1, has_south)

        @pl.when(has_north)
        def _():
            for copy in halo(0):
                copy.wait_send()

        @pl.when(has_south)
        def _():
            for copy in halo(1):
                copy.wait_send()

    def surface_sides(q):
        for copy in side_copies(q):
            copy.wait_recv()
        place_edges(
            surf,
            inside(q),
            [side_recv[q, 0, piece] for piece in range(pieces)],
            [side_recv[q, 1, piece] for piece in range(pieces)],
        )

    def slope_step(low, high):
        @pl.loop(low, high, unroll=True)
        def _(i):
            at, up, down = strip_rows(i, 0), strip_rows(i, -1), strip_rows(i, 1)
            slope_x = sides(rows_of(surf, 2, at))
            for j in range(every):
                slope_y = 0.5 * (surf[2, j, down, :] - surf[2, j, up, :])
                gain = -0.5 * fields[MASS, j, at, :]
                fields[WX, j, at, :] = fields[WX, j, at, :] + gain * slope_x[j]
                fields[WY, j, at, :] = fields[WY, j, at, :] + gain * slope_y

    halves = 2 * SUB - 1

    def half_step(h, low, high):
        if h == halves - 1:
            low, high = max(low, 1), min(high, all_strips - 1)
        low, high = max(low, 0), min(high, all_strips)
        if low >= high:
            return
        if h == 0:
            slope_step(low, high)
        if h % 2:
            stress_step(False, low, high)
        else:
            velocity_step(low, high, tiles if h == halves - 1 else every)

    late_low = 1 + order[-1] * chunk_strips - 1
    late_high = 1 + (order[-1] + 1) * chunk_strips + 1

    def early_steps(first, last):
        for h in range(first, last):
            half_step(h, 0, late_low - h)
            half_step(h, late_high + h, all_strips)

    def late_steps():
        for h in range(halves):
            half_step(h, late_low - h, late_high + h)

    for n, q in enumerate(order):
        for t in cross:
            need(0, t, q)
            cross_message(t, q, False)
        if n and order[n - 1] not in traded:
            send_p(order[n - 1])
        for t in cross:
            cross_message(t, q, True)
        if n == 0:
            statics()
            for late in traded:
                for i in others:
                    send_y(i, 0, late, [arrived(gets["a", i, late])])
                    start_y(i, 0, late)
        if n == CHUNKS // 2:
            field_halo()
        if n >= 2:
            surface(order[n - 2])
    if order[-1] not in traded:
        send_p(order[-1])
    first_stress()
    surface(order[-2])
    for q in order[:-2]:
        surface_sides(q)
    surface_sides(order[-2])
    for send_sem, source in ((send_sems.at[0], send_codes), (send_sems.at[1], send_scales)):
        remote(source, source, send_sem, recv_sems.at[0, 0], mate).wait_send()
    surface(order[-1])
    surface_halo()
    early_steps(0, halves)
    surface_sides(order[-1])
    late_steps()
    remote(side_send, side_recv, side_sends_sem, side_sems.at[0, 0], west).wait_send()


def write_out(fields, stress, vel_out, stress_out, sems):
    tiles = fields.shape[1] - 1
    rows = pl.ds(2 * HALO, vel_out.shape[1])
    copies = []
    for j in range(tiles):
        cols = pl.ds(j * LANES, LANES)
        for n, (source, target) in enumerate(
            ((fields.at[pl.ds(U, 2)], vel_out), (stress, stress_out))
        ):
            copy = pltpu.make_async_copy(
                source.at[:, j, rows, :], target.at[:, :, cols], sems.at[n, j]
            )
            copy.start()
            copies.append(copy)
    for copy in copies:
        copy.wait()


def body(
    ocean, level_weight, velocity_start, wind_stress, thickness, concentration, ice_mask, land_mask
):
    secs, rows_g, cols_g = lax.axis_size("sec"), lax.axis_size("gy"), lax.axis_size("gx")
    held = ocean.shape[0]
    rows, cols = thickness.shape
    tiles = cols // LANES
    tall = rows + 4 * HALO
    wide_rows = rows + 2 * HALO
    size = rows // CHUNKS
    pieces = pl.cdiv(3 * (size // 8), LANES // HALO)
    field_pieces = pl.cdiv(FIELDS * (wide_rows // 8), LANES // HALO)
    f32, i16 = jnp.float32, jnp.int16
    dma = pltpu.SemaphoreType.DMA
    anywhere = pl.BlockSpec(memory_space=pl.ANY)
    on_chip = pl.BlockSpec(memory_space=pltpu.VMEM)
    sends, gets = numbered(secs, rows_g)
    fields, stress = pl.pallas_call(
        functools.partial(kernel, (secs, rows_g, cols_g, level_weight.shape[0])),
        out_shape=(
            pltpu.VMEM((FIELDS, tiles + 1, tall, LANES), f32),
            pltpu.VMEM((3, tiles + 1, tall, LANES), f32),
        ),
        in_specs=[anywhere] * 8,
        out_specs=(on_chip, on_chip),
        scratch_shapes=[
            pltpu.VMEM((secs * rows_g, held, 3, rows, cols), ocean.dtype),
            pltpu.VMEM((len(sends), 3, size, cols), i16),
            pltpu.VMEM((len(sends), 3, LANES), f32),
            pltpu.VMEM((len(gets), 3, size, cols), i16),
            pltpu.VMEM((len(gets), 3, LANES), f32),
            pltpu.VMEM((2, rows, cols), f32),
            pltpu.VMEM((2, rows, cols), f32),
            pltpu.VMEM((rows, cols), f32),
            pltpu.VMEM((rows, cols), f32),
            pltpu.VMEM((rows, cols), jnp.int32),
            pltpu.VMEM((rows, cols), jnp.int32),
            pltpu.VMEM((3, tiles + 1, tall, LANES), f32),
            pltpu.VMEM((2, FIELDS * HALO, cols), i16),
            pltpu.VMEM((2, FIELDS, LANES), f32),
            pltpu.VMEM((2, FIELDS * HALO, cols), i16),
            pltpu.VMEM((2, FIELDS, LANES), f32),
            pltpu.VMEM((2, field_pieces, 8, LANES), f32),
            pltpu.VMEM((2, field_pieces, 8, LANES), f32),
            pltpu.VMEM((2, 3, tiles, HALO, LANES), f32),
            pltpu.VMEM((2, 3, tiles, HALO, LANES), f32),
            pltpu.VMEM((CHUNKS, 2, pieces, 8, LANES), f32),
            pltpu.VMEM((CHUNKS, 2, pieces, 8, LANES), f32),
            pltpu.VMEM((2, 2, 3, HALO, LANES), f32),
            pltpu.SMEM(level_weight.shape, f32),
            dma(()),
            dma((secs - 1, rows_g - 2)),
            dma((secs * rows_g,)),
            dma((6,)),
            dma((2,)),
            dma((len(gets), 2)),
            dma((2, 2, 2)),
            dma((2, 2)),
            dma((2, 3, 2)),
            dma(()),
            dma((CHUNKS, 2)),
            pltpu.SemaphoreType.REGULAR((rows_g,)),
        ],
        compiler_params=pltpu.CompilerParams(
            collective_id=0, has_side_effects=True, vmem_limit_bytes=52 * 1024 * 1024
        ),
    )(
        level_weight,
        ocean,
        velocity_start,
        wind_stress,
        thickness,
        concentration,
        ice_mask,
        land_mask,
    )
    return pl.pallas_call(
        write_out,
        out_shape=(
            jax.ShapeDtypeStruct((2, rows, cols), f32),
            jax.ShapeDtypeStruct((3, rows, cols), f32),
        ),
        in_specs=[on_chip, on_chip],
        out_specs=(anywhere, anywhere),
        scratch_shapes=[dma((2, tiles))],
        compiler_params=pltpu.CompilerParams(vmem_limit_bytes=VMEM_OUT),
    )(fields, stress)


def solution(mesh):
    placed = (
        P(("sec", "gy"), None, None, "gx"),
        P(),
        P(None, ("sec", "gy"), "gx"),
        P(None, ("sec", "gy"), "gx"),
        P(("sec", "gy"), "gx"),
        P(("sec", "gy"), "gx"),
        P(("sec", "gy"), "gx"),
        P(("sec", "gy"), "gx"),
    )
    return jax.shard_map(
        body,
        mesh=mesh,
        in_specs=placed,
        out_specs=(P(None, ("sec", "gy"), "gx"), P(None, ("sec", "gy"), "gx")),
        check_vma=False,
    )
```
